256 devices in a mesh: sym: 4 (over z_hi, core), dev: 64 (over y, z_lo, x).
Axes of the slice: x: 4, y: 4, z: 8 (z_hi: 2, z_lo: 4; z = z_hi * 4 + z_lo), core: 2. Of those that a mesh axis runs over, the one named last changes fastest.
Arguments:
- inner_state: float32 [8, 2, 4096], P('sym', None, 'dev'), may hold values from -6 to 6
- block_sizes: int32 [8], replicated, may hold values from 1024 to 4096, as said below
- block_ham: bfloat16 [8, 4096, 4096], P('sym', 'dev'), as said below
- dipole_inner: bfloat16 [8, 4096, 4096], P('sym', 'dev'), may hold values from -0.09375 to 0.09375
- surface_amps: bfloat16 [800, 4096], P(None, 'dev'), may hold values from -0.29882812 to 0.29882812
- channel_block: int32 [800, 1], replicated, may hold values from 0 to 7
- outer_state: float32 [2, 800, 32768], P(None, None, ('sym', 'dev')), may hold values from -6 to 6
- channel_energy: float32 [800], replicated, may hold values from 2 to 40
- laser_dipole: bfloat16 [800, 800], replicated, as said below
Outputs:
- inner_next: float32 [8, 2, 4096], P('sym', None, 'dev')
- outer_next: float32 [2, 800, 32768], P(None, None, ('sym', 'dev'))
The draws below stay inside these ranges and needn't reach their ends.
Inputs may be any that keep to these rules, and one draw needn't show every extreme that they name: `block_sizes`: live states of each block; some block has exactly 4096. `channel_block`: every block has at least one channel. `block_ham`: each block is a symmetric matrix. `laser_dipole`: Symmetric.
All inputs are finite; a program needn't handle non-finite values.
Results may differ from the reference program's by a relative error of at most 0.0035.
Values may be sent and summed in bfloat16 or wider, within the bound.
A program may use at most 64 MiB of HBM per device.

```python
import math
import jax
import jax.numpy as jnp
from jax import lax

NCH = 800
MAXB = 4096
BLOCKS = 8
TERMS = 4
STEPS = 1
NR = 32768


def draw_block_sizes(key, part):
    first_key, second_key = jax.random.split(jax.random.fold_in(key, 3))
    sizes_drawn = jax.random.randint(first_key, (BLOCKS,), MAXB // 4, MAXB + 1, dtype=jnp.int32)
    largest = jax.random.randint(second_key, (), 0, BLOCKS, dtype=jnp.int32)
    return jnp.where(jnp.arange(BLOCKS, dtype=jnp.int32) == largest, MAXB, sizes_drawn).astype(jnp.int32)


def normal_square(single, order):
    sample = jax.random.normal(single, (order, order), jnp.float32)
    return (sample + sample.T) * 0.5 ** 0.5 / order ** 0.5


def draw_block_ham(key, part):
    block_keys = jax.random.split(jax.random.fold_in(key, 11), BLOCKS)
    blocks = lax.map(lambda single: normal_square(single, MAXB), block_keys)
    return blocks.astype(jnp.bfloat16)


def draw_laser_dipole(key, part):
    matrix_key = jax.random.fold_in(key, 23)
    matrix = normal_square(matrix_key, NCH)
    return matrix.astype(jnp.bfloat16)


def block_levels(own_key, shape, cuts, least, top_value):
    gain = 1.0
    for position, blocks in cuts:
        steps = jax.random.uniform(jax.random.fold_in(jax.random.fold_in(own_key, 6), position), (blocks,), jnp.float32, least / len(cuts), top_value / len(cuts))
        gain = gain * jnp.repeat(jnp.exp(steps), shape[position] // blocks).reshape((-1,) + (1,) * (len(shape) - 1 - position))
    return gain


def distinct(stream_key, rows, amount, top, lift):
    sequence = jax.random.permutation(jax.random.fold_in(stream_key, 1), amount)
    pull = sequence
    for power in range(3):
        pull = pull * pull // amount
    pull = pull * lift // amount
    tickets = jax.random.randint(jax.random.fold_in(stream_key, 2), (rows, amount), 0, 4096) + pull
    holders = jax.random.permutation(jax.random.fold_in(stream_key, 3), rows)[jnp.arange(amount) % rows]
    tickets = jnp.where(jnp.arange(rows)[:, None] == holders[None, :], 1 << 14, tickets)
    merit = tickets * amount + jnp.arange(amount)
    return lax.top_k(merit.astype(jnp.int32), top)[1].astype(jnp.int32)


def normal_values(stream_key, dims, width, reach, cuts=(), kind=jnp.bfloat16):
    gain = block_levels(stream_key, dims, cuts, -0.22, 0.18) if cuts else 1.0
    array = jax.random.normal(stream_key, dims, jnp.float32) * width * gain
    return jnp.minimum(jnp.maximum(array, -reach), reach).astype(kind)


def setup_inputs(seed: int = 0) -> dict:
    arg_keys = jax.random.split(jax.random.key(seed), 10)
    inner_state = normal_values(arg_keys[0], (BLOCKS, 2, MAXB), 1.0, 6.0, ((0, 4), (2, 64)), jnp.float32)
    block_sizes = draw_block_sizes(jax.random.fold_in(arg_keys[9], 71), 0)
    block_ham = draw_block_ham(jax.random.fold_in(arg_keys[9], 71), 0)
    dipole_inner = normal_values(arg_keys[3], (BLOCKS, MAXB, MAXB), MAXB ** -0.5, 0.09375, ((0, 4), (1, 64)))
    surface_amps = normal_values(arg_keys[4], (NCH, MAXB), 0.05, 0.29882812, ((1, 64),))
    channel_block = distinct(arg_keys[5], NCH, BLOCKS, 1, 0)
    outer_state = normal_values(arg_keys[6], (2, NCH, NR), 1.0, 6.0, ((2, 256),), jnp.float32)
    channel_energy = jnp.clip(jnp.exp(jax.random.uniform(arg_keys[7], (NCH,), jnp.float32, math.log(2.0), math.log(40.0))), 2.0, 40.0)
    laser_dipole = draw_laser_dipole(jax.random.fold_in(arg_keys[9], 71), 0)
    return dict(inner_state=inner_state, block_sizes=block_sizes, block_ham=block_ham, dipole_inner=dipole_inner, surface_amps=surface_amps, channel_block=channel_block, outer_state=outer_state, channel_energy=channel_energy, laser_dipole=laser_dipole)


time_step = 0.012
spacing = 0.1
kinetic = 0.5 / (spacing * spacing)
block_scale = 90.0
dipole_scale = 40.0
laser_scale = 25.0


def inner_products(state_half, block_ham, dipole_inner):
    def per_block(pieces):
        matrix, coupling, own_block, next_state = pieces
        diagonal_part = jnp.dot(matrix, own_block.T, preferred_element_type=jnp.float32).T
        forward = jnp.dot(coupling, next_state.T, preferred_element_type=jnp.float32).T
        backward = jnp.dot(own_block, coupling, preferred_element_type=jnp.float32)
        return diagonal_part, forward, backward

    zero_block = jnp.zeros((1, 2, MAXB), jnp.bfloat16)
    next_states = jnp.concatenate([state_half[1:], zero_block], axis=0)
    diagonal_part, forward, backward = lax.map(per_block, (block_ham, dipole_inner, state_half, next_states))
    lower_part = jnp.concatenate([jnp.zeros((1, 2, MAXB), jnp.float32), backward[:-1]], axis=0)
    return diagonal_part, forward, lower_part


def reference(inner_state, block_sizes, block_ham, dipole_inner, surface_amps, channel_block, outer_state, channel_energy, laser_dipole):
    positions = jnp.arange(MAXB, dtype=jnp.int32)
    live_rows = (positions[None, :] < block_sizes[:, None])[:, None, :]
    owners = channel_block[:, 0].astype(jnp.int32)
    onehot = (owners[None, :] == jnp.arange(BLOCKS, dtype=jnp.int32)[:, None]).astype(jnp.float32)
    amps_wide = surface_amps.astype(jnp.float32)
    dipole_wide = laser_dipole.astype(jnp.float32)
    inner_now = jnp.where(live_rows, inner_state, jnp.float32(0.0))
    outer_now = outer_state
    for period in range(STEPS):
        inner_sum = inner_now
        outer_sum = outer_now
        inner_term = inner_now
        outer_term = outer_now
        for degree in range(1, TERMS + 1):
            factor = time_step / degree
            state_half = inner_term.astype(jnp.bfloat16)
            slope_half = ((-3.0 * outer_term[:, :, 0] + 4.0 * outer_term[:, :, 1] - outer_term[:, :, 2]) * (0.5 / spacing)).astype(jnp.bfloat16)
            chosen = state_half.astype(jnp.float32)[owners]
            boundary = jnp.einsum("cr,cir->ic", amps_wide, chosen)
            masked = onehot[:, None, :] * slope_half.astype(jnp.float32)[None]
            bloch_term = jnp.einsum("bic,cr->bir", masked, amps_wide)
            diagonal_part, forward, lower_part = inner_products(state_half, block_ham, dipole_inner)
            image = jnp.where(live_rows, block_scale * diagonal_part + dipole_scale * (forward + lower_part) + bloch_term, jnp.float32(0.0))
            inner_term = factor * jnp.stack([image[:, 1], -image[:, 0]], axis=1)
            inner_sum = inner_sum + inner_term
            right_cells = jnp.zeros((2, NCH, 1), jnp.float32)
            extended = jnp.concatenate([boundary[:, :, None], outer_term, right_cells], axis=2)
            curvature = extended[:, :, :-2] - 2.0 * extended[:, :, 1:-1] + extended[:, :, 2:]
            rounded = lax.optimization_barrier(outer_term.astype(jnp.bfloat16)).astype(jnp.float32)
            mixed_term = jnp.einsum("cd,idn->icn", dipole_wide, rounded)
            outer_image = -kinetic * curvature + channel_energy[None, :, None] * outer_term + laser_scale * mixed_term
            outer_term = factor * jnp.stack([outer_image[1], -outer_image[0]])
            outer_sum = outer_sum + outer_term
        inner_now = inner_sum
        outer_now = outer_sum
    return inner_now, outer_now
```

```python
import functools

import jax
import jax.numpy as jnp
from jax import lax
from jax.experimental import pallas as pl
from jax.experimental.pallas import tpu as pltpu
from jax.sharding import PartitionSpec as P

TERMS = 4
time_step = 0.012
spacing = 0.1
kinetic = 0.5 / (spacing * spacing)
block_scale = 90.0
dipole_scale = 40.0
laser_scale = 25.0

MESH = pl.DeviceIdType.MESH
F32, BF16 = jnp.float32, jnp.bfloat16
NT = (((1,), (1,)), ((), ()))

SYM, DEV = 4, 64
TOP = 8


def torus(step):
    return min(step, 4 - step)


OFFSETS = sorted(
    [(oy, ox) for oy in range(4) for ox in range(4) if (oy, ox) != (0, 0)],
    key=lambda o: -(torus(o[0]) + torus(o[1])),
)


def remote(src, dst, send, recv, sym, dev):
    return pltpu.make_async_remote_copy(
        src_ref=src, dst_ref=dst, send_sem=send, recv_sem=recv, device_id=(sym, dev), device_id_type=MESH
    )


def drain(ref, sem):
    pltpu.make_async_copy(ref, ref, sem).wait()


def kernel(
    sizes, inner, ham, dip, amps, chan, outer, energy, laser,
    inner_out, outer_out,
    inn, mats, dips, ampv, chv, out_raw, env, lasv, u, acc, wst, wsum,
    stage1, got1, stage2, own, stage3, above, stage4, below,
    bst, bgot, bst2, bgot2, sgot,
    load, store, halo_send, halo_recv, send1, recv1, send2, recv2, send3, recv3, send4, recv4,
    bsend, brecv, bsend2, brecv2, ssend, srecv, ssend2,
):
    s = lax.axis_index("sym")
    d = lax.axis_index("dev")
    y, zl, x = d // 16, (d // 4) % 4, d % 4
    plane = y * 4 + x
    parity = x % 2
    group = s * 4 + zl
    is_plane_root = plane == 0
    is_root = jnp.logical_and(s == 0, d == 0)
    is_last = jnp.logical_and(s == SYM - 1, d == DEV - 1)
    channels = ampv.shape[1]
    points = out_raw.shape[2]
    rows = u.shape[1]

    def dev_of(y_, z_, x_):
        return (y_ * 4 + z_) * 4 + x_

    loads = [
        pltpu.make_async_copy(inner, inn, load.at[0]),
        pltpu.make_async_copy(dip, dips, load.at[1]),
        pltpu.make_async_copy(amps, ampv, load.at[2]),
        pltpu.make_async_copy(chan, chv, load.at[3]),
        pltpu.make_async_copy(outer, out_raw, load.at[4]),
        pltpu.make_async_copy(energy, env, load.at[5]),
        pltpu.make_async_copy(laser, lasv, load.at[6]),
        pltpu.make_async_copy(ham, mats, load.at[7]),
    ]
    for one in loads:
        one.start()

    barrier = pltpu.get_barrier_semaphore()

    def greet(sym, dev):
        pl.semaphore_signal(barrier, inc=1, device_id=(sym, dev), device_id_type=MESH)

    for oy, ox in OFFSETS:
        greet(s, dev_of((y + oy) % 4, zl, (x + ox) % 4))
    for oz in range(1, 4):
        greet(s, dev_of(y, (zl + oz) % 4, x))
    expected = jnp.int32(18)
    has_below = s > 0
    has_above = s < SYM - 1

    @pl.when(has_below)
    def _():
        for z_ in range(4):
            greet(s - 1, dev_of(y, z_, x))

    @pl.when(has_above)
    def _():
        for z_ in range(4):
            greet(s + 1, dev_of(y, z_, x))

    expected += 4 * has_below.astype(jnp.int32) + 4 * has_above.astype(jnp.int32)

    @pl.when(is_root)
    def _():
        for g in range(1, 16):
            greet(jnp.int32(g // 4), jnp.int32((g % 4) * 4))

    hears_root = jnp.logical_and(is_plane_root, jnp.logical_not(is_root))

    @pl.when(hears_root)
    def _():
        greet(jnp.int32(0), jnp.int32(0))

    expected += 15 * is_root.astype(jnp.int32) + hears_root.astype(jnp.int32)
    position = s * DEV + d
    left, right = position - 1, position + 1
    has_left = jnp.logical_not(is_root)
    has_right = jnp.logical_not(is_last)

    @pl.when(has_left)
    def _():
        greet(left // DEV, left % DEV)

    @pl.when(has_right)
    def _():
        greet(right // DEV, right % DEV)

    expected += has_left.astype(jnp.int32) + has_right.astype(jnp.int32)

    loads[0].wait()
    size0, size1 = sizes[2 * s], sizes[2 * s + 1]
    row_index = d * 64 + lax.broadcasted_iota(jnp.int32, (2, 64), 1)
    live0 = row_index < size0
    live1 = row_index < size1
    first = jnp.concatenate(
        [jnp.where(live0, inn[0], 0.0), jnp.where(live1, inn[1], 0.0)], axis=0
    )
    wst[...] = first
    wsum[...] = first
    for one in loads[2:6]:
        one.wait()
    blank = jnp.zeros((2, TOP, channels), F32)

    @pl.when(is_root)
    def _():
        u[:, 0:TOP, :] = blank

    @pl.when(is_last)
    def _():
        u[:, TOP + points : rows, :] = blank

    for i in range(2):
        turned = jnp.transpose(out_raw[i])
        u[i, TOP : TOP + points, :] = turned
        acc[i] = turned

    def slope_of(i):
        near = u[i, TOP : TOP + 8, :]
        return (-3.0 * near[0:1] + 4.0 * near[1:2] - near[2:3]) * (0.5 / spacing)

    def stage_slope(k):
        both = jnp.concatenate([slope_of(0), slope_of(1)], axis=0)
        sgot[k] = both.astype(BF16)

    @pl.when(is_root)
    def _():
        stage_slope(0)

    pl.semaphore_wait(barrier, expected)

    to_left = remote(
        u.at[:, pl.ds(TOP, 8), :], u.at[:, pl.ds(TOP + points, 8), :],
        halo_send.at[0], halo_recv.at[0], left // DEV, left % DEV,
    )
    to_right = remote(
        u.at[:, pl.ds(points, 8), :], u.at[:, pl.ds(0, 8), :],
        halo_send.at[1], halo_recv.at[1], right // DEV, right % DEV,
    )

    @pl.when(has_left)
    def _():
        to_left.start()

    @pl.when(has_right)
    def _():
        to_right.start()

    loads[1].wait()
    owned0 = (chv[...] == 2 * s).astype(F32)
    owned1 = (chv[...] == 2 * s + 1).astype(F32)
    zero64 = jnp.zeros((2, 64), BF16)
    line = lax.broadcasted_iota(jnp.int32, (rows, 1), 0)
    inside = jnp.logical_and(
        jnp.logical_or(line >= TOP, has_left), jnp.logical_or(line < TOP + points, has_right)
    )

    def slope_to(k, g):
        return remote(
            sgot.at[k], sgot.at[k], ssend.at[g], srecv.at[k], jnp.int32(g // 4), jnp.int32((g % 4) * 4)
        )

    def slope_on(k, n):
        oy, ox = OFFSETS[n]
        return remote(sgot.at[k], sgot.at[k], ssend2.at[n], srecv.at[k], s, dev_of(oy, zl, ox))

    @pl.loop(0, TERMS)
    def _(k):
        factor = time_step / (k + 1).astype(F32)
        half = wst[...].astype(BF16)

        spread = jnp.concatenate(
            [jnp.concatenate([half[0:2], zero64], axis=1), jnp.concatenate([zero64, half[2:4]], axis=1)], axis=0
        )
        flat = dips[...].reshape(128, dips.shape[2])
        part = jnp.dot(spread, flat, preferred_element_type=F32).astype(BF16)
        zero4 = jnp.zeros((4, 64), BF16)
        even = jnp.concatenate([half, zero4], axis=1)
        odd = jnp.concatenate([zero4, half], axis=1)
        chunk = jnp.where(parity == 0, even, odd)
        for y_ in range(4):
            for xh in range(2):
                stage1[y_ * 2 + xh, 0] = chunk
                for z_ in range(4):
                    tile = (y_ * 4 + z_) * 2 + xh
                    stage1[y_ * 2 + xh, 1 + z_] = part[:, tile * 128 : (tile + 1) * 128]
        sends1 = []
        for n, (oy, ox) in enumerate(OFFSETS):
            ty, tx = (y + oy) % 4, (x + ox) % 4
            sends1.append(
                remote(
                    stage1.at[ty * 2 + tx // 2], got1.at[k, plane], send1, recv1.at[k], s, dev_of(ty, zl, tx)
                )
            )
            sends1[-1].start()

        @pl.when(is_root)
        def _():
            for g in range(1, 16):
                slope_to(k, g).start()

        per_block = jnp.dot(half, ampv[...], preferred_element_type=F32)
        bound = owned0 * per_block[0:2] + owned1 * per_block[2:4]

        @pl.when(is_plane_root)
        def _():
            bgot[k, 0] = bound

        @pl.when(jnp.logical_not(is_plane_root))
        def _():
            bst[...] = bound
            remote(bst, bgot.at[k, plane], bsend, brecv.at[k], s, dev_of(0, zl, 0)).start()

        got1[k, plane] = stage1[y * 2 + x // 2]
        drain(got1.at[k, pl.ds(0, 15)], recv1.at[k])

        sums = got1[k, 0, 1:5].astype(F32)
        for p in range(1, 16):
            sums += got1[k, p, 1:5].astype(F32)
        sums = sums.astype(BF16)
        pairs = [got1[k, 2 * q, 0] + got1[k, 2 * q + 1, 0] for q in range(8)]
        for z_ in range(4):
            for q in range(8):
                stage2[z_, q] = pairs[q]
            stage2[z_, 8] = sums[z_]
            stage4[z_] = sums[z_]
        for q in range(8):
            stage3[q] = pairs[q][0:2]
        for oz in (2, 1, 3):
            tz = (zl + oz) % 4
            remote(stage2.at[tz], own.at[k, zl], send2, recv2.at[k], s, dev_of(y, tz, x)).start()

        @pl.when(has_below)
        def _():
            for z_ in range(4):
                remote(stage3, above.at[k, zl], send3, recv3.at[k], s - 1, dev_of(y, z_, x)).start()

        @pl.when(has_above)
        def _():
            for z_ in range(4):
                remote(stage4.at[z_], below.at[k, zl], send4, recv4.at[k], s + 1, dev_of(y, z_, x)).start()

        own[k, zl] = stage2[zl]

        @pl.when(is_plane_root)
        def _():
            drain(bgot.at[k, pl.ds(0, 15)], brecv.at[k])
            total = jnp.sum(bgot[k], axis=0)

            @pl.when(is_root)
            def _():
                bgot2[k, 0] = total

            @pl.when(jnp.logical_not(is_root))
            def _():
                bst2[...] = total
                remote(bst2, bgot2.at[k, group], bsend2, brecv2.at[k], jnp.int32(0), jnp.int32(0)).start()
                drain(sgot.at[k], srecv.at[k])

            for n in range(15):
                slope_on(k, n).start()

        @pl.when(k == 0)
        def _():
            @pl.when(has_left)
            def _():
                to_right.wait_recv()
                to_left.wait_send()

            @pl.when(has_right)
            def _():
                to_left.wait_recv()
                to_right.wait_send()

            loads[6].wait()
            loads[7].wait()

        images = []
        for i in range(2):
            value = u[i]
            mixed = jnp.dot(value.astype(BF16), lasv[...], preferred_element_type=F32)
            curve = pltpu.roll(value, 1, 0) - 2.0 * value + pltpu.roll(value, rows - 1, 0)
            image = -kinetic * curve + env[...] * value + laser_scale * mixed
            images.append(jnp.where(inside, image, 0.0))
        new0 = factor * images[1]
        new1 = -factor * images[0]
        u[0] = new0
        u[1] = new1
        acc[0] += new0[TOP : TOP + points]
        acc[1] += new1[TOP : TOP + points]

        @pl.when(jnp.logical_not(is_plane_root))
        def _():
            drain(sgot.at[k], srecv.at[k])

        slope = sgot[k].astype(F32)
        masked = jnp.concatenate([owned0 * slope, owned1 * slope], axis=0).astype(BF16)
        bloch = lax.dot_general(masked, ampv[...], NT, preferred_element_type=F32)

        drain(own.at[k, pl.ds(0, 3)], recv2.at[k])

        @pl.when(has_above)
        def _():
            drain(above.at[k], recv3.at[k])

        @pl.when(has_below)
        def _():
            drain(below.at[k], recv4.at[k])

        order = [(y_, z_, xh) for y_ in range(4) for z_ in range(4) for xh in range(2)]
        mine = jnp.concatenate([own[k, z_, y_ * 2 + xh] for y_, z_, xh in order], axis=1)
        upper = jnp.concatenate([above[k, z_, y_ * 2 + xh] for y_, z_, xh in order], axis=1)

        def times(vectors, matrix):
            return lax.dot_general(vectors, matrix, NT, preferred_element_type=F32)

        diag0 = times(mine, mats[0])[0:2]
        diag1 = times(mine, mats[1])[2:4]
        forward0 = times(mine, dips[0])[2:4]
        forward1 = jnp.where(has_above, times(upper, dips[1]), 0.0)

        def half_of(tile):
            return jnp.where(parity == 0, tile[:, 0:64], tile[:, 64:128])

        lower0 = below[k, 0].astype(F32)
        lower1 = own[k, 0, 8].astype(F32)
        for z_ in range(1, 4):
            lower0 += below[k, z_].astype(F32)
            lower1 += own[k, z_, 8].astype(F32)
        lower0 = jnp.where(has_below, half_of(lower0)[2:4], 0.0)
        lower1 = half_of(lower1)[0:2]
        image0 = block_scale * diag0 + dipole_scale * (forward0 + lower0) + bloch[0:2]
        image1 = block_scale * diag1 + dipole_scale * (forward1 + lower1) + bloch[2:4]
        image0 = jnp.where(live0, image0, 0.0)
        image1 = jnp.where(live1, image1, 0.0)
        fresh = factor * jnp.concatenate([image0[1:2], -image0[0:1], image1[1:2], -image1[0:1]], axis=0)
        wst[...] = fresh
        wsum[...] += fresh

        @pl.when(is_root)
        def _():
            drain(bgot2.at[k, pl.ds(0, 15)], brecv2.at[k])
            edge = (-kinetic) * jnp.sum(bgot2[k], axis=0)
            fix0 = factor * edge[1:2]
            fix1 = -factor * edge[0:1]
            u[0, TOP : TOP + 1, :] += fix0
            u[1, TOP : TOP + 1, :] += fix1
            acc[0, 0:1, :] += fix0
            acc[1, 0:1, :] += fix1

            @pl.when(k < TERMS - 1)
            def _():
                stage_slope(k + 1)

        drain(got1.at[k, pl.ds(0, 15)], send1)
        drain(own.at[k, pl.ds(0, 3)], send2)

        @pl.when(has_below)
        def _():
            drain(above.at[k], send3)

        @pl.when(has_above)
        def _():
            drain(below.at[k], send4)

        @pl.when(jnp.logical_not(is_plane_root))
        def _():
            drain(bst, bsend)

        @pl.when(is_plane_root)
        def _():
            for n in range(15):
                slope_on(k, n).wait_send()

        @pl.when(is_root)
        def _():
            for g in range(1, 16):
                slope_to(k, g).wait_send()

        @pl.when(hears_root)
        def _():
            drain(bst2, bsend2)

    inner_out[0] = wsum[0:2]
    inner_out[1] = wsum[2:4]
    for i in range(2):
        out_raw[i] = jnp.transpose(acc[i])
    last = pltpu.make_async_copy(out_raw, outer_out, store)
    last.start()
    last.wait()


def on_device(inner, sizes, ham, dip, amps, chan, outer, energy, laser):
    blocks, parts, own_rows = inner.shape
    states = ham.shape[2]
    channels, points = outer.shape[1], outer.shape[2]
    rows = points + 16
    dma = pltpu.SemaphoreType.DMA
    anywhere = pl.BlockSpec(memory_space=pl.ANY)
    return pl.pallas_call(
        kernel,
        out_shape=(
            jax.ShapeDtypeStruct(inner.shape, F32),
            jax.ShapeDtypeStruct(outer.shape, F32),
        ),
        in_specs=[pl.BlockSpec(memory_space=pltpu.SMEM)] + [anywhere] * 8,
        out_specs=(pl.BlockSpec(memory_space=pltpu.VMEM), anywhere),
        scratch_shapes=[
            pltpu.VMEM(inner.shape, F32),
            pltpu.VMEM(ham.shape, BF16),
            pltpu.VMEM(dip.shape, BF16),
            pltpu.VMEM((own_rows, channels), BF16),
            pltpu.VMEM((1, channels), jnp.int32),
            pltpu.VMEM(outer.shape, F32),
            pltpu.VMEM((1, channels), F32),
            pltpu.VMEM(laser.shape, BF16),
            pltpu.VMEM((2, rows, channels), F32),
            pltpu.VMEM((2, points, channels), F32),
            pltpu.VMEM((4, own_rows), F32),
            pltpu.VMEM((4, own_rows), F32),
            pltpu.VMEM((8, 5, 4, 128), BF16),
            pltpu.VMEM((TERMS, 16, 5, 4, 128), BF16),
            pltpu.VMEM((4, 9, 4, 128), BF16),
            pltpu.VMEM((TERMS, 4, 9, 4, 128), BF16),
            pltpu.VMEM((8, 2, 128), BF16),
            pltpu.VMEM((TERMS, 4, 8, 2, 128), BF16),
            pltpu.VMEM((4, 4, 128), BF16),
            pltpu.VMEM((TERMS, 4, 4, 128), BF16),
            pltpu.VMEM((2, channels), F32),
            pltpu.VMEM((TERMS, 16, 2, channels), F32),
            pltpu.VMEM((2, channels), F32),
            pltpu.VMEM((TERMS, 16, 2, channels), F32),
            pltpu.VMEM((TERMS, 2, channels), BF16),
            dma((8,)), dma, dma((2,)), dma((2,)),
            dma, dma((TERMS,)), dma, dma((TERMS,)), dma, dma((TERMS,)), dma, dma((TERMS,)),
            dma, dma((TERMS,)), dma, dma((TERMS,)), dma((16,)), dma((TERMS,)), dma((15,)),
        ],
        compiler_params=pltpu.CompilerParams(
            collective_id=0, has_side_effects=True, vmem_limit_bytes=60 * 1024 * 1024
        ),
    )(
        sizes, inner, ham, dip, amps.T, chan.reshape(1, channels), outer, energy.reshape(1, channels), laser,
    )


def solution(mesh):
    placed = (
        P("sym", None, "dev"),
        P(),
        P("sym", "dev", None),
        P("sym", "dev", None),
        P(None, "dev"),
        P(),
        P(None, None, ("sym", "dev")),
        P(),
        P(),
    )
    return jax.shard_map(
        on_device,
        mesh=mesh,
        in_specs=placed,
        out_specs=(P("sym", None, "dev"), P(None, None, ("sym", "dev"))),
        check_vma=False,
    )
```

```python
import functools

import jax
import jax.numpy as jnp
from jax import lax
from jax.experimental import pallas as pl
from jax.experimental.pallas import tpu as pltpu
from jax.sharding import PartitionSpec as P

TERMS = 4
time_step = 0.012
spacing = 0.1
kinetic = 0.5 / (spacing * spacing)
block_scale = 90.0
dipole_scale = 40.0
laser_scale = 25.0

MESH = pl.DeviceIdType.MESH
F32, BF16 = jnp.float32, jnp.bfloat16
NT = (((1,), (1,)), ((), ()))

SYM, DEV = 4, 64
TOP = 8


def torus(step):
    return min(step, 4 - step)


OFFSETS = sorted(
    [(oy, ox) for oy in range(4) for ox in range(4) if (oy, ox) != (0, 0)],
    key=lambda o: -(torus(o[0]) + torus(o[1])),
)


def remote(src, dst, send, recv, sym, dev):
    return pltpu.make_async_remote_copy(
        src_ref=src, dst_ref=dst, send_sem=send, recv_sem=recv, device_id=(sym, dev), device_id_type=MESH
    )


def drain(ref, sem):
    pltpu.make_async_copy(ref, ref, sem).wait()


def kernel(
    sizes_in, inner, ham, dip, amps, chan, outer, energy, laser,
    inner_out, outer_out,
    sizes, inn, mats, dips, ampv, chv, out_raw, env, lasv, u, acc, wsum,
    stage1, got1, stage2, own, stage3, above, stage4, below,
    bst, bgot, bst2, bgot2, sgot,
    load, halo_send, halo_recv, send1, recv1, send2, recv2, send3, recv3, send4, recv4,
    bsend, brecv, bsend2, brecv2, ssend, srecv, ssend2,
):
    s = lax.axis_index("sym")
    d = lax.axis_index("dev")
    y, zl, x = d // 16, (d // 4) % 4, d % 4
    plane = y * 4 + x
    parity = x % 2
    group = s * 4 + zl
    is_plane_root = plane == 0
    is_root = jnp.logical_and(s == 0, d == 0)
    is_last = jnp.logical_and(s == SYM - 1, d == DEV - 1)
    channels = ampv.shape[1]
    points = out_raw.shape[2]
    rows = u.shape[1]

    def dev_of(y_, z_, x_):
        return (y_ * 4 + z_) * 4 + x_

    barrier = pltpu.get_barrier_semaphore()

    def greet(sym, dev):
        pl.semaphore_signal(barrier, inc=1, device_id=(sym, dev), device_id_type=MESH)

    for oy, ox in OFFSETS:
        greet(s, dev_of((y + oy) % 4, zl, (x + ox) % 4))
    for oz in range(1, 4):
        greet(s, dev_of(y, (zl + oz) % 4, x))
    expected = jnp.int32(18)
    has_below = s > 0
    has_above = s < SYM - 1

    @pl.when(has_below)
    def _():
        for z_ in range(4):
            greet(s - 1, dev_of(y, z_, x))

    @pl.when(has_above)
    def _():
        for z_ in range(4):
            greet(s + 1, dev_of(y, z_, x))

    expected += 4 * has_below.astype(jnp.int32) + 4 * has_above.astype(jnp.int32)

    @pl.when(is_root)
    def _():
        for g in range(1, 16):
            greet(jnp.int32(g // 4), jnp.int32((g % 4) * 4))

    hears_root = jnp.logical_and(is_plane_root, jnp.logical_not(is_root))

    @pl.when(hears_root)
    def _():
        greet(jnp.int32(0), jnp.int32(0))

    expected += 15 * is_root.astype(jnp.int32) + hears_root.astype(jnp.int32)
    position = s * DEV + d
    left, right = position - 1, position + 1
    has_left = jnp.logical_not(is_root)
    has_right = jnp.logical_not(is_last)

    @pl.when(has_left)
    def _():
        greet(left // DEV, left % DEV)

    @pl.when(has_right)
    def _():
        greet(right // DEV, right % DEV)

    expected += has_left.astype(jnp.int32) + has_right.astype(jnp.int32)

    pairs = (
        (sizes_in, sizes), (inner, inn), (dip, dips), (amps, ampv), (chan, chv),
        (outer, out_raw), (energy, env), (laser, lasv), (ham, mats),
    )
    loads = [pltpu.make_async_copy(src, dst, load.at[n]) for n, (src, dst) in enumerate(pairs)]
    for one in loads:
        one.start()

    for one in loads[0:3]:
        one.wait()
    size0, size1 = sizes[2 * s], sizes[2 * s + 1]
    row_index = d * 64 + lax.broadcasted_iota(jnp.int32, (2, 64), 1)
    live0 = row_index < size0
    live1 = row_index < size1
    zero2 = jnp.zeros((2, 64), BF16)
    zero4 = jnp.zeros((4, 64), BF16)

    def prepare(state):
        half = state.astype(BF16)
        spread = jnp.concatenate(
            [jnp.concatenate([half[0:2], zero2], axis=1), jnp.concatenate([zero2, half[2:4]], axis=1)], axis=0
        )
        flat = dips[...].reshape(128, dips.shape[2])
        part = jnp.dot(spread, flat, preferred_element_type=F32).astype(BF16)
        even = jnp.concatenate([half, zero4], axis=1)
        odd = jnp.concatenate([zero4, half], axis=1)
        chunk = jnp.where(parity == 0, even, odd)
        for y_ in range(4):
            for xh in range(2):
                stage1[y_ * 2 + xh, 0] = chunk
                for z_ in range(4):
                    tile = (y_ * 4 + z_) * 2 + xh
                    stage1[y_ * 2 + xh, 1 + z_] = part[:, tile * 128 : (tile + 1) * 128]
        per_block = jnp.dot(half, ampv[...], preferred_element_type=F32)
        bst[...] = owned0 * per_block[0:2] + owned1 * per_block[2:4]

    first = jnp.concatenate(
        [jnp.where(live0, inn[0], 0.0), jnp.where(live1, inn[1], 0.0)], axis=0
    )
    wsum[...] = first
    loads[3].wait()
    loads[4].wait()
    owned0 = (chv[...] == 2 * s).astype(F32)
    owned1 = (chv[...] == 2 * s + 1).astype(F32)
    prepare(first)

    loads[5].wait()
    blank = jnp.zeros((2, TOP, channels), F32)

    @pl.when(is_root)
    def _():
        u[:, 0:TOP, :] = blank

    @pl.when(is_last)
    def _():
        u[:, TOP + points : rows, :] = blank

    for i in range(2):
        turned = jnp.transpose(out_raw[i])
        u[i, TOP : TOP + points, :] = turned
        acc[i] = turned

    def slope_of(i):
        near = u[i, TOP : TOP + 8, :]
        return (-3.0 * near[0:1] + 4.0 * near[1:2] - near[2:3]) * (0.5 / spacing)

    def stage_slope(k):
        both = jnp.concatenate([slope_of(0), slope_of(1)], axis=0)
        sgot[k] = both.astype(BF16)

    @pl.when(is_root)
    def _():
        stage_slope(0)

    for one in loads[6:9]:
        one.wait()
    line = lax.broadcasted_iota(jnp.int32, (rows, 1), 0)
    inside = jnp.logical_and(
        jnp.logical_or(line >= TOP, has_left), jnp.logical_or(line < TOP + points, has_right)
    )

    to_left = remote(
        u.at[:, pl.ds(TOP, 8), :], u.at[:, pl.ds(TOP + points, 8), :],
        halo_send.at[0], halo_recv.at[0], left // DEV, left % DEV,
    )
    to_right = remote(
        u.at[:, pl.ds(points, 8), :], u.at[:, pl.ds(0, 8), :],
        halo_send.at[1], halo_recv.at[1], right // DEV, right % DEV,
    )

    def slope_to(k, g):
        return remote(
            sgot.at[k], sgot.at[k], ssend.at[g], srecv.at[k], jnp.int32(g // 4), jnp.int32((g % 4) * 4)
        )

    def slope_on(k, n):
        oy, ox = OFFSETS[n]
        return remote(sgot.at[k], sgot.at[k], ssend2.at[n], srecv.at[k], s, dev_of(oy, zl, ox))

    def close_grid(k):
        drain(bgot2.at[k, pl.ds(0, 15)], brecv2.at[k])
        edge = jnp.sum(bgot2[k], axis=0) * (-kinetic * time_step / (k + 1).astype(F32))
        u[0, TOP : TOP + 1, :] += edge[1:2]
        u[1, TOP : TOP + 1, :] -= edge[0:1]
        acc[0, 0:1, :] += edge[1:2]
        acc[1, 0:1, :] -= edge[0:1]

    pl.semaphore_wait(barrier, expected)

    @pl.loop(0, TERMS)
    def _(k):
        factor = time_step / (k + 1).astype(F32)

        for n, (oy, ox) in enumerate(OFFSETS):
            ty, tx = (y + oy) % 4, (x + ox) % 4
            remote(
                stage1.at[ty * 2 + tx // 2], got1.at[k, plane], send1, recv1.at[k], s, dev_of(ty, zl, tx)
            ).start()

        @pl.when(jnp.logical_not(is_plane_root))
        def _():
            remote(bst, bgot.at[k, plane], bsend, brecv.at[k], s, dev_of(0, zl, 0)).start()

        @pl.when(is_root)
        def _():
            @pl.when(k > 0)
            def _():
                close_grid(k - 1)
                stage_slope(k)

            for g in range(1, 16):
                slope_to(k, g).start()

        @pl.when(k == 0)
        def _():
            @pl.when(has_left)
            def _():
                to_left.start()

            @pl.when(has_right)
            def _():
                to_right.start()

        got1[k, plane] = stage1[y * 2 + x // 2]

        @pl.when(is_plane_root)
        def _():
            bgot[k, 0] = bst[...]

        drain(got1.at[k, pl.ds(0, 15)], recv1.at[k])

        sums = got1[k, 0, 1:5].astype(F32)
        for p in range(1, 16):
            sums += got1[k, p, 1:5].astype(F32)
        sums = sums.astype(BF16)
        pairs = [got1[k, 2 * q, 0] + got1[k, 2 * q + 1, 0] for q in range(8)]
        for z_ in range(4):
            for q in range(8):
                stage2[z_, q] = pairs[q]
            stage2[z_, 8] = sums[z_]
            stage4[z_] = sums[z_]
        for q in range(8):
            stage3[q] = pairs[q][0:2]

        @pl.when(has_below)
        def _():
            for z_ in range(4):
                remote(stage3, above.at[k, zl], send3, recv3.at[k], s - 1, dev_of(y, z_, x)).start()

        @pl.when(has_above)
        def _():
            for z_ in range(4):
                remote(stage4.at[z_], below.at[k, zl], send4, recv4.at[k], s + 1, dev_of(y, z_, x)).start()

        for oz in (2, 1, 3):
            tz = (zl + oz) % 4
            remote(stage2.at[tz], own.at[k, zl], send2, recv2.at[k], s, dev_of(y, tz, x)).start()
        own[k, zl] = stage2[zl]

        @pl.when(is_plane_root)
        def _():
            drain(bgot.at[k, pl.ds(0, 15)], brecv.at[k])
            total = jnp.sum(bgot[k], axis=0)

            @pl.when(is_root)
            def _():
                bgot2[k, 0] = total

            @pl.when(jnp.logical_not(is_root))
            def _():
                bst2[...] = total
                remote(bst2, bgot2.at[k, group], bsend2, brecv2.at[k], jnp.int32(0), jnp.int32(0)).start()
                drain(sgot.at[k], srecv.at[k])

            for n in range(15):
                slope_on(k, n).start()

        @pl.when(k == 0)
        def _():
            @pl.when(has_left)
            def _():
                to_right.wait_recv()
                to_left.wait_send()

            @pl.when(has_right)
            def _():
                to_left.wait_recv()
                to_right.wait_send()

        images = []
        levels = env[...].reshape(1, channels)
        for i in range(2):
            value = u[i]
            mixed = jnp.dot(value.astype(BF16), lasv[...], preferred_element_type=F32)
            curve = pltpu.roll(value, 1, 0) - 2.0 * value + pltpu.roll(value, rows - 1, 0)
            image = -kinetic * curve + levels * value + laser_scale * mixed
            images.append(jnp.where(inside, image, 0.0))
        new0 = factor * images[1]
        new1 = -factor * images[0]
        u[0] = new0
        u[1] = new1
        acc[0] += new0[TOP : TOP + points]
        acc[1] += new1[TOP : TOP + points]

        @pl.when(jnp.logical_and(k == TERMS - 1, jnp.logical_not(is_root)))
        def _():
            for i in range(2):
                outer_out[i] = jnp.transpose(acc[i])

        drain(own.at[k, pl.ds(0, 3)], recv2.at[k])

        @pl.when(has_above)
        def _():
            drain(above.at[k], recv3.at[k])

        @pl.when(has_below)
        def _():
            drain(below.at[k], recv4.at[k])

        order = [(y_, z_, xh) for y_ in range(4) for z_ in range(4) for xh in range(2)]
        mine = jnp.concatenate([own[k, z_, y_ * 2 + xh] for y_, z_, xh in order], axis=1)
        upper = jnp.concatenate([above[k, z_, y_ * 2 + xh] for y_, z_, xh in order], axis=1)

        def times(vectors, matrix):
            return lax.dot_general(vectors, matrix, NT, preferred_element_type=F32)

        diag0 = times(mine, mats[0])[0:2]
        diag1 = times(mine, mats[1])[2:4]
        forward0 = times(mine, dips[0])[2:4]
        forward1 = jnp.where(has_above, times(upper, dips[1]), 0.0)

        def half_of(tile):
            return jnp.where(parity == 0, tile[:, 0:64], tile[:, 64:128])

        lower0 = below[k, 0].astype(F32)
        lower1 = own[k, 0, 8].astype(F32)
        for z_ in range(1, 4):
            lower0 += below[k, z_].astype(F32)
            lower1 += own[k, z_, 8].astype(F32)
        lower0 = jnp.where(has_below, half_of(lower0)[2:4], 0.0)
        lower1 = half_of(lower1)[0:2]
        image0 = block_scale * diag0 + dipole_scale * (forward0 + lower0)
        image1 = block_scale * diag1 + dipole_scale * (forward1 + lower1)

        @pl.when(jnp.logical_not(is_plane_root))
        def _():
            drain(sgot.at[k], srecv.at[k])

        slope = sgot[k].astype(F32)
        masked = jnp.concatenate([owned0 * slope, owned1 * slope], axis=0).astype(BF16)
        bloch = lax.dot_general(masked, ampv[...], NT, preferred_element_type=F32)
        image0 = jnp.where(live0, image0 + bloch[0:2], 0.0)
        image1 = jnp.where(live1, image1 + bloch[2:4], 0.0)
        fresh = factor * jnp.concatenate([image0[1:2], -image0[0:1], image1[1:2], -image1[0:1]], axis=0)
        wsum[...] += fresh

        drain(got1.at[k, pl.ds(0, 15)], send1)
        drain(own.at[k, pl.ds(0, 3)], send2)

        @pl.when(has_below)
        def _():
            drain(above.at[k], send3)

        @pl.when(has_above)
        def _():
            drain(below.at[k], send4)

        @pl.when(jnp.logical_not(is_plane_root))
        def _():
            drain(bst, bsend)

        @pl.when(k < TERMS - 1)
        def _():
            prepare(fresh)

        @pl.when(is_plane_root)
        def _():
            for n in range(15):
                slope_on(k, n).wait_send()

        @pl.when(is_root)
        def _():
            for g in range(1, 16):
                slope_to(k, g).wait_send()

        @pl.when(hears_root)
        def _():
            drain(bst2, bsend2)

    inner_out[0] = wsum[0:2]
    inner_out[1] = wsum[2:4]

    @pl.when(is_root)
    def _():
        close_grid(jnp.int32(TERMS - 1))
        for i in range(2):
            outer_out[i] = jnp.transpose(acc[i])


def deliver(inner_v, outer_v, inner_out, outer_out, sems):
    copies = [
        pltpu.make_async_copy(outer_v, outer_out, sems.at[0]),
        pltpu.make_async_copy(inner_v, inner_out, sems.at[1]),
    ]
    for one in copies:
        one.start()
    for one in copies:
        one.wait()


def on_device(inner, sizes, ham, dip, amps, chan, outer, energy, laser):
    blocks, parts, own_rows = inner.shape
    states = ham.shape[2]
    channels, points = outer.shape[1], outer.shape[2]
    rows = points + 16
    dma = pltpu.SemaphoreType.DMA
    anywhere = pl.BlockSpec(memory_space=pl.ANY)
    results = pl.pallas_call(
        kernel,
        out_shape=(
            pltpu.VMEM(inner.shape, F32),
            pltpu.VMEM(outer.shape, F32),
        ),
        in_specs=[anywhere] * 9,
        out_specs=(pl.BlockSpec(memory_space=pltpu.VMEM), pl.BlockSpec(memory_space=pltpu.VMEM)),
        scratch_shapes=[
            pltpu.SMEM(sizes.shape, jnp.int32),
            pltpu.VMEM(inner.shape, F32),
            pltpu.VMEM(ham.shape, BF16),
            pltpu.VMEM(dip.shape, BF16),
            pltpu.VMEM((own_rows, channels), BF16),
            pltpu.VMEM((1, channels), jnp.int32),
            pltpu.VMEM(outer.shape, F32),
            pltpu.VMEM((channels,), F32),
            pltpu.VMEM(laser.shape, BF16),
            pltpu.VMEM((2, rows, channels), F32),
            pltpu.VMEM((2, points, channels), F32),
            pltpu.VMEM((4, own_rows), F32),
            pltpu.VMEM((8, 5, 4, 128), BF16),
            pltpu.VMEM((TERMS, 16, 5, 4, 128), BF16),
            pltpu.VMEM((4, 9, 4, 128), BF16),
            pltpu.VMEM((TERMS, 4, 9, 4, 128), BF16),
            pltpu.VMEM((8, 2, 128), BF16),
            pltpu.VMEM((TERMS, 4, 8, 2, 128), BF16),
            pltpu.VMEM((4, 4, 128), BF16),
            pltpu.VMEM((TERMS, 4, 4, 128), BF16),
            pltpu.VMEM((2, channels), F32),
            pltpu.VMEM((TERMS, 16, 2, channels), F32),
            pltpu.VMEM((2, channels), F32),
            pltpu.VMEM((TERMS, 16, 2, channels), F32),
            pltpu.VMEM((TERMS, 2, channels), BF16),
            dma((9,)), dma((2,)), dma((2,)),
            dma, dma((TERMS,)), dma, dma((TERMS,)), dma, dma((TERMS,)), dma, dma((TERMS,)),
            dma, dma((TERMS,)), dma, dma((TERMS,)), dma((16,)), dma((TERMS,)), dma((15,)),
        ],
        compiler_params=pltpu.CompilerParams(
            collective_id=0, has_side_effects=True, vmem_limit_bytes=60 * 1024 * 1024
        ),
    )(
        sizes, inner, ham, dip, amps.T, chan.reshape(1, channels), outer, energy, laser,
    )
    return pl.pallas_call(
        deliver,
        out_shape=(
            jax.ShapeDtypeStruct(inner.shape, F32),
            jax.ShapeDtypeStruct(outer.shape, F32),
        ),
        in_specs=[pl.BlockSpec(memory_space=pltpu.VMEM)] * 2,
        out_specs=(anywhere, anywhere),
        scratch_shapes=[dma((2,))],
        compiler_params=pltpu.CompilerParams(vmem_limit_bytes=1024 * 1024),
    )(*results)


def solution(mesh):
    placed = (
        P("sym", None, "dev"),
        P(),
        P("sym", "dev", None),
        P("sym", "dev", None),
        P(None, "dev"),
        P(),
        P(None, None, ("sym", "dev")),
        P(),
        P(),
    )
    return jax.shard_map(
        on_device,
        mesh=mesh,
        in_specs=placed,
        out_specs=(P("sym", None, "dev"), P(None, None, ("sym", "dev"))),
        check_vma=False,
    )
```

```python
import functools

import jax
import jax.numpy as jnp
from jax import lax
from jax.experimental import pallas as pl
from jax.experimental.pallas import tpu as pltpu
from jax.sharding import PartitionSpec as P

TERMS = 4
time_step = 0.012
spacing = 0.1
kinetic = 0.5 / (spacing * spacing)
block_scale = 90.0
dipole_scale = 40.0
laser_scale = 25.0

MESH = pl.DeviceIdType.MESH
F32, BF16 = jnp.float32, jnp.bfloat16
NT = (((1,), (1,)), ((), ()))

SYM, DEV = 4, 64
TOP = 8


def torus(step):
    return min(step, 4 - step)


OFFSETS = sorted(
    [(oy, ox) for oy in range(4) for ox in range(4) if (oy, ox) != (0, 0)],
    key=lambda o: -(torus(o[0]) + torus(o[1])),
)


def remote(src, dst, send, recv, sym, dev):
    return pltpu.make_async_remote_copy(
        src_ref=src, dst_ref=dst, send_sem=send, recv_sem=recv, device_id=(sym, dev), device_id_type=MESH
    )


def drain(ref, sem):
    pltpu.make_async_copy(ref, ref, sem).wait()


def kernel(
    sizes_in, inner, ham, dip, amps, chan, outer, energy, laser,
    inner_out, outer_out,
    sizes, inn, mats, dips, ampv, chv, out_raw, env, lasv, u, acc, wsum,
    stage1, got1, stage2, own, stage3, above, stage4, below,
    staged, first2, got, above_d, below_d, lows, highs, lower_h, upper_h,
    bst, bgot, bst2, bgot2, sgot,
    load, halo_send, halo_recv, send1, recv1, send2, recv2, send3, recv3, send4, recv4,
    sendd, recvd, sendx, recvx, sendh, recvh,
    bsend, brecv, bsend2, brecv2, ssend, srecv, ssend2,
):
    s = lax.axis_index("sym")
    d = lax.axis_index("dev")
    y, zl, x = d // 16, (d // 4) % 4, d % 4
    plane = y * 4 + x
    parity = x % 2
    group = s * 4 + zl
    is_plane_root = plane == 0
    is_root = jnp.logical_and(s == 0, d == 0)
    is_last = jnp.logical_and(s == SYM - 1, d == DEV - 1)
    channels = ampv.shape[1]
    points = out_raw.shape[2]
    rows = u.shape[1]

    def dev_of(y_, z_, x_):
        return (y_ * 4 + z_) * 4 + x_

    barrier = pltpu.get_barrier_semaphore()

    def greet(sym, dev):
        pl.semaphore_signal(barrier, inc=1, device_id=(sym, dev), device_id_type=MESH)

    for oy, ox in OFFSETS:
        greet(s, dev_of((y + oy) % 4, zl, (x + ox) % 4))
    for oz in range(1, 4):
        greet(s, dev_of(y, (zl + oz) % 4, x))
    expected = jnp.int32(18)
    has_below = s > 0
    has_above = s < SYM - 1

    @pl.when(has_below)
    def _():
        for z_ in range(4):
            greet(s - 1, dev_of(y, z_, x))

    @pl.when(has_above)
    def _():
        for z_ in range(4):
            greet(s + 1, dev_of(y, z_, x))

    expected += 4 * has_below.astype(jnp.int32) + 4 * has_above.astype(jnp.int32)

    @pl.when(is_root)
    def _():
        for g in range(1, 16):
            greet(jnp.int32(g // 4), jnp.int32((g % 4) * 4))

    hears_root = jnp.logical_and(is_plane_root, jnp.logical_not(is_root))

    @pl.when(hears_root)
    def _():
        greet(jnp.int32(0), jnp.int32(0))

    expected += 15 * is_root.astype(jnp.int32) + hears_root.astype(jnp.int32)
    position = s * DEV + d
    left, right = position - 1, position + 1
    has_left = jnp.logical_not(is_root)
    has_right = jnp.logical_not(is_last)

    @pl.when(has_left)
    def _():
        greet(left // DEV, left % DEV)

    @pl.when(has_right)
    def _():
        greet(right // DEV, right % DEV)

    expected += has_left.astype(jnp.int32) + has_right.astype(jnp.int32)

    pairs = (
        (sizes_in, sizes), (inner, inn), (dip, dips), (amps, ampv), (chan, chv),
        (outer, out_raw), (energy, env), (laser, lasv), (ham, mats),
    )
    loads = [pltpu.make_async_copy(src, dst, load.at[n]) for n, (src, dst) in enumerate(pairs)]
    for one in loads:
        one.start()

    for one in loads[0:3]:
        one.wait()
    size0, size1 = sizes[2 * s], sizes[2 * s + 1]
    row_index = d * 64 + lax.broadcasted_iota(jnp.int32, (2, 64), 1)
    live0 = row_index < size0
    live1 = row_index < size1
    zero2 = jnp.zeros((2, 64), BF16)
    zero4 = jnp.zeros((4, 64), BF16)

    def products(state):
        half = state.astype(BF16)
        spread = jnp.concatenate(
            [jnp.concatenate([half[0:2], zero2], axis=1), jnp.concatenate([zero2, half[2:4]], axis=1)], axis=0
        )
        flat = dips[...].reshape(128, dips.shape[2])
        part = jnp.dot(spread, flat, preferred_element_type=F32).astype(BF16)
        even = jnp.concatenate([half, zero4], axis=1)
        odd = jnp.concatenate([zero4, half], axis=1)
        chunk = jnp.where(parity == 0, even, odd)
        per_block = jnp.dot(half, ampv[...], preferred_element_type=F32)
        bst[...] = owned0 * per_block[0:2] + owned1 * per_block[2:4]
        return chunk, part

    def prepare_plane(state):
        chunk, part = products(state)
        for y_ in range(4):
            for xh in range(2):
                stage1[y_ * 2 + xh, 0] = chunk
                for z_ in range(4):
                    tile = (y_ * 4 + z_) * 2 + xh
                    stage1[y_ * 2 + xh, 1 + z_] = part[:, tile * 128 : (tile + 1) * 128]

    def prepare_direct(state):
        chunk, part = products(state)
        first2[...] = chunk[0:2]
        for tile in range(32):
            staged[tile, 0] = chunk
            staged[tile, 1] = part[:, tile * 128 : (tile + 1) * 128]

    first = jnp.concatenate(
        [jnp.where(live0, inn[0], 0.0), jnp.where(live1, inn[1], 0.0)], axis=0
    )
    wsum[...] = first
    loads[3].wait()
    loads[4].wait()
    owned0 = (chv[...] == 2 * s).astype(F32)
    owned1 = (chv[...] == 2 * s + 1).astype(F32)
    prepare_plane(first)

    loads[5].wait()
    blank = jnp.zeros((2, TOP, channels), F32)

    @pl.when(is_root)
    def _():
        u[:, 0:TOP, :] = blank

    @pl.when(is_last)
    def _():
        u[:, TOP + points : rows, :] = blank

    for i in range(2):
        turned = jnp.transpose(out_raw[i])
        u[i, TOP : TOP + points, :] = turned
        acc[i] = turned

    def slope_of(i):
        near = u[i, TOP : TOP + 8, :]
        return (-3.0 * near[0:1] + 4.0 * near[1:2] - near[2:3]) * (0.5 / spacing)

    def stage_slope(k):
        both = jnp.concatenate([slope_of(0), slope_of(1)], axis=0)
        sgot[k] = both.astype(BF16)

    @pl.when(is_root)
    def _():
        stage_slope(0)

    for one in loads[6:9]:
        one.wait()
    line = lax.broadcasted_iota(jnp.int32, (rows, 1), 0)
    inside = jnp.logical_and(
        jnp.logical_or(line >= TOP, has_left), jnp.logical_or(line < TOP + points, has_right)
    )

    to_left = remote(
        u.at[:, pl.ds(TOP, 8), :], u.at[:, pl.ds(TOP + points, 8), :],
        halo_send.at[0], halo_recv.at[0], left // DEV, left % DEV,
    )
    to_right = remote(
        u.at[:, pl.ds(points, 8), :], u.at[:, pl.ds(0, 8), :],
        halo_send.at[1], halo_recv.at[1], right // DEV, right % DEV,
    )

    def slope_to(k, g):
        return remote(
            sgot.at[k], sgot.at[k], ssend.at[g], srecv.at[k], jnp.int32(g // 4), jnp.int32((g % 4) * 4)
        )

    def slope_on(k, n):
        oy, ox = OFFSETS[n]
        return remote(sgot.at[k], sgot.at[k], ssend2.at[n], srecv.at[k], s, dev_of(oy, zl, ox))

    def factor_of(k):
        return time_step / (k + 1) if isinstance(k, int) else time_step / (k + 1).astype(F32)

    def close_grid(k):
        drain(bgot2.at[k, pl.ds(0, 15)], brecv2.at[k])
        edge = jnp.sum(bgot2[k], axis=0) * (-kinetic * factor_of(k))
        u[0, TOP : TOP + 1, :] += edge[1:2]
        u[1, TOP : TOP + 1, :] -= edge[0:1]
        acc[0, 0:1, :] += edge[1:2]
        acc[1, 0:1, :] -= edge[0:1]

    def send_boundary(k):
        @pl.when(is_plane_root)
        def _():
            bgot[k, 0] = bst[...]

        @pl.when(jnp.logical_not(is_plane_root))
        def _():
            remote(bst, bgot.at[k, plane], bsend, brecv.at[k], s, dev_of(0, zl, 0)).start()

    def send_slope(k):
        for g in range(1, 16):
            slope_to(k, g).start()

    def relay(k):
        @pl.when(hears_root)
        def _():
            drain(sgot.at[k], srecv.at[k])

        for n in range(15):
            slope_on(k, n).start()
        drain(bgot.at[k, pl.ds(0, 15)], brecv.at[k])
        total = jnp.sum(bgot[k], axis=0)

        @pl.when(is_root)
        def _():
            bgot2[k, 0] = total

        @pl.when(hears_root)
        def _():
            bst2[...] = total
            remote(bst2, bgot2.at[k, group], bsend2, brecv2.at[k], jnp.int32(0), jnp.int32(0)).start()

    def outer_update(k):
        factor = factor_of(k)
        images = []
        levels = env[...].reshape(1, channels)
        for i in range(2):
            value = u[i]
            mixed = jnp.dot(value.astype(BF16), lasv[...], preferred_element_type=F32)
            curve = pltpu.roll(value, 1, 0) - 2.0 * value + pltpu.roll(value, rows - 1, 0)
            image = -kinetic * curve + levels * value + laser_scale * mixed
            images.append(jnp.where(inside, image, 0.0))
        new0 = factor * images[1]
        new1 = -factor * images[0]
        u[0] = new0
        u[1] = new1
        acc[0] += new0[TOP : TOP + points]
        acc[1] += new1[TOP : TOP + points]

    def times(vectors, matrix):
        return lax.dot_general(vectors, matrix, NT, preferred_element_type=F32)

    def half_of(tile):
        return jnp.where(parity == 0, tile[:, 0:64], tile[:, 64:128])

    def finish(k, image0, image1):
        @pl.when(jnp.logical_not(is_plane_root))
        def _():
            drain(sgot.at[k], srecv.at[k])

        slope = sgot[k].astype(F32)
        masked = jnp.concatenate([owned0 * slope, owned1 * slope], axis=0).astype(BF16)
        bloch = lax.dot_general(masked, ampv[...], NT, preferred_element_type=F32)
        image0 = jnp.where(live0, image0 + bloch[0:2], 0.0)
        image1 = jnp.where(live1, image1 + bloch[2:4], 0.0)
        fresh = factor_of(k) * jnp.concatenate(
            [image0[1:2], -image0[0:1], image1[1:2], -image1[0:1]], axis=0
        )
        wsum[...] += fresh

        @pl.when(jnp.logical_not(is_plane_root))
        def _():
            drain(bst, bsend)

        return fresh

    def sent_slope(k):
        @pl.when(is_plane_root)
        def _():
            for n in range(15):
                slope_on(k, n).wait_send()

        @pl.when(is_root)
        def _():
            for g in range(1, 16):
                slope_to(k, g).wait_send()

        @pl.when(hears_root)
        def _():
            drain(bst2, bsend2)

    pl.semaphore_wait(barrier, expected)

    for n, (oy, ox) in enumerate(OFFSETS):
        ty, tx = (y + oy) % 4, (x + ox) % 4
        remote(
            stage1.at[ty * 2 + tx // 2], got1.at[plane], send1, recv1, s, dev_of(ty, zl, tx)
        ).start()
    send_boundary(0)

    @pl.when(is_root)
    def _():
        send_slope(0)

    @pl.when(has_left)
    def _():
        to_left.start()

    @pl.when(has_right)
    def _():
        to_right.start()

    got1[plane] = stage1[y * 2 + x // 2]
    drain(got1.at[pl.ds(0, 15)], recv1)

    sums = got1[0, 1:5].astype(F32)
    for p in range(1, 16):
        sums += got1[p, 1:5].astype(F32)
    sums = sums.astype(BF16)
    tiles = [got1[2 * q, 0] + got1[2 * q + 1, 0] for q in range(8)]
    for z_ in range(4):
        for q in range(8):
            stage2[z_, q] = tiles[q]
        stage2[z_, 8] = sums[z_]
        stage4[z_] = sums[z_]
    for q in range(8):
        stage3[q] = tiles[q][0:2]

    @pl.when(has_below)
    def _():
        for z_ in range(4):
            remote(stage3, above.at[zl], send3, recv3, s - 1, dev_of(y, z_, x)).start()

    @pl.when(has_above)
    def _():
        for z_ in range(4):
            remote(stage4.at[z_], below.at[zl], send4, recv4, s + 1, dev_of(y, z_, x)).start()

    for oz in (2, 1, 3):
        tz = (zl + oz) % 4
        remote(stage2.at[tz], own.at[zl], send2, recv2, s, dev_of(y, tz, x)).start()
    own[zl] = stage2[zl]

    @pl.when(is_plane_root)
    def _():
        relay(0)

    @pl.when(has_left)
    def _():
        to_right.wait_recv()
        to_left.wait_send()

    @pl.when(has_right)
    def _():
        to_left.wait_recv()
        to_right.wait_send()

    outer_update(0)

    @pl.when(is_root)
    def _():
        close_grid(0)
        stage_slope(1)
        send_slope(1)

    drain(own.at[pl.ds(0, 3)], recv2)

    @pl.when(has_above)
    def _():
        drain(above, recv3)

    @pl.when(has_below)
    def _():
        drain(below, recv4)

    order = [(y_, z_, xh) for y_ in range(4) for z_ in range(4) for xh in range(2)]
    mine = jnp.concatenate([own[z_, y_ * 2 + xh] for y_, z_, xh in order], axis=1)
    upper = jnp.concatenate([above[z_, y_ * 2 + xh] for y_, z_, xh in order], axis=1)
    lower0 = below[0].astype(F32)
    lower1 = own[0, 8].astype(F32)
    for z_ in range(1, 4):
        lower0 += below[z_].astype(F32)
        lower1 += own[z_, 8].astype(F32)
    lower0 = jnp.where(has_below, half_of(lower0)[2:4], 0.0)
    lower1 = half_of(lower1)[0:2]
    forward1 = jnp.where(has_above, times(upper, dips[1]), 0.0)
    image0 = block_scale * times(mine, mats[0])[0:2] + dipole_scale * (times(mine, dips[0])[2:4] + lower0)
    image1 = block_scale * times(mine, mats[1])[2:4] + dipole_scale * (forward1 + lower1)
    fresh = finish(0, image0, image1)
    prepare_direct(fresh)
    drain(got1.at[pl.ds(0, 15)], send1)
    drain(own.at[pl.ds(0, 3)], send2)

    @pl.when(has_below)
    def _():
        drain(above, send3)

    @pl.when(has_above)
    def _():
        drain(below, send4)

    sent_slope(0)
    partner = s + 1 - 2 * (s % 2)
    is_low = s % 2 == 0
    is_high = s % 2 == 1

    @pl.loop(1, TERMS)
    def _(k):
        send_boundary(k)
        for level in range(4, -1, -1):
            ring = [o for o in OFFSETS + [(0, 0)] if torus(o[0]) + torus(o[1]) == level]
            targets = [
                (dev_of((y + oy) % 4, (zl + oz) % 4, (x + ox) % 4), (oy, oz, ox)) for oz in (2, 1, 3, 0) for oy, ox in ring
            ]

            @pl.when(s == 1)
            def _():
                for to, _o in targets:
                    remote(staged.at[to // 2, 1], below_d.at[k, d], sendx, recvx.at[k], jnp.int32(2), to).start()

            @pl.when(s == 2)
            def _():
                for to, _o in targets:
                    remote(first2, above_d.at[k, d], sendx, recvx.at[k], jnp.int32(1), to).start()

            for to, offset in targets:
                if offset != (0, 0, 0):
                    remote(staged.at[to // 2], got.at[k, d], sendd, recvd.at[k], s, to).start()

        got[k, d] = staged[d // 2]

        @pl.when(is_plane_root)
        def _():
            relay(k)

        outer_update(k)

        @pl.when(jnp.logical_and(k == TERMS - 1, jnp.logical_not(is_root)))
        def _():
            for i in range(2):
                outer_out[i] = jnp.transpose(acc[i])

        @pl.when(jnp.logical_and(is_root, k < TERMS - 1))
        def _():
            close_grid(k)
            stage_slope(k + 1)
            send_slope(k + 1)

        drain(got.at[k, pl.ds(0, 63)], recvd.at[k])
        sums = got[k, 0, 1].astype(F32)
        for p in range(1, 64):
            sums += got[k, p, 1].astype(F32)
        mine = jnp.concatenate([got[k, 2 * q, 0] + got[k, 2 * q + 1, 0] for q in range(32)], axis=1)

        give_low = remote(lows, lower_h.at[k], sendh, recvh.at[k], partner, d)
        give_high = remote(highs, upper_h.at[k], sendh, recvh.at[k], partner, d)

        @pl.when(is_low)
        def _():
            lows[...] = sums[2:4]
            give_low.start()

        @pl.when(is_high)
        def _():
            highs[...] = mine[0:2]
            give_high.start()

        image0 = block_scale * times(mine, mats[0])[0:2] + dipole_scale * times(mine, dips[0])[2:4]
        image1 = block_scale * times(mine, mats[1])[2:4] + dipole_scale * half_of(sums)[0:2]

        @pl.when(s == 1)
        def _():
            drain(above_d.at[k], recvx.at[k])
            for q in range(32):
                upper_h[k, :, q * 128 : (q + 1) * 128] = above_d[k, 2 * q] + above_d[k, 2 * q + 1]

        @pl.when(s == 2)
        def _():
            drain(below_d.at[k], recvx.at[k])
            total = below_d[k, 0].astype(F32)
            for p in range(1, 64):
                total += below_d[k, p].astype(F32)
            lower_h[k] = total[2:4]

        @pl.when(is_low)
        def _():
            drain(upper_h.at[k], recvh.at[k])

        @pl.when(is_high)
        def _():
            drain(lower_h.at[k], recvh.at[k])

        image0 += jnp.where(has_below, dipole_scale * half_of(lower_h[k]), 0.0)
        image1 += jnp.where(has_above, dipole_scale * times(upper_h[k], dips[1]), 0.0)
        fresh = finish(k, image0, image1)

        drain(got.at[k, pl.ds(0, 63)], sendd)

        @pl.when(s == 1)
        def _():
            drain(below_d.at[k], sendx)

        @pl.when(s == 2)
        def _():
            drain(above_d.at[k], sendx)

        @pl.when(k < TERMS - 1)
        def _():
            prepare_direct(fresh)

        @pl.when(is_low)
        def _():
            drain(lower_h.at[k], sendh)

        @pl.when(is_high)
        def _():
            drain(upper_h.at[k], sendh)

        sent_slope(k)

    inner_out[0] = wsum[0:2]
    inner_out[1] = wsum[2:4]

    @pl.when(is_root)
    def _():
        close_grid(TERMS - 1)
        for i in range(2):
            outer_out[i] = jnp.transpose(acc[i])


def deliver(inner_v, outer_v, inner_out, outer_out, sems):
    copies = [
        pltpu.make_async_copy(outer_v, outer_out, sems.at[0]),
        pltpu.make_async_copy(inner_v, inner_out, sems.at[1]),
    ]
    for one in copies:
        one.start()
    for one in copies:
        one.wait()


def on_device(inner, sizes, ham, dip, amps, chan, outer, energy, laser):
    blocks, parts, own_rows = inner.shape
    states = ham.shape[2]
    channels, points = outer.shape[1], outer.shape[2]
    rows = points + 16
    dma = pltpu.SemaphoreType.DMA
    anywhere = pl.BlockSpec(memory_space=pl.ANY)
    results = pl.pallas_call(
        kernel,
        out_shape=(
            pltpu.VMEM(inner.shape, F32),
            pltpu.VMEM(outer.shape, F32),
        ),
        in_specs=[anywhere] * 9,
        out_specs=(pl.BlockSpec(memory_space=pltpu.VMEM), pl.BlockSpec(memory_space=pltpu.VMEM)),
        scratch_shapes=[
            pltpu.SMEM(sizes.shape, jnp.int32),
            pltpu.VMEM(inner.shape, F32),
            pltpu.VMEM(ham.shape, BF16),
            pltpu.VMEM(dip.shape, BF16),
            pltpu.VMEM((own_rows, channels), BF16),
            pltpu.VMEM((1, channels), jnp.int32),
            pltpu.VMEM(outer.shape, F32),
            pltpu.VMEM((channels,), F32),
            pltpu.VMEM(laser.shape, BF16),
            pltpu.VMEM((2, rows, channels), F32),
            pltpu.VMEM((2, points, channels), F32),
            pltpu.VMEM((4, own_rows), F32),
            pltpu.VMEM((8, 5, 4, 128), BF16),
            pltpu.VMEM((16, 5, 4, 128), BF16),
            pltpu.VMEM((4, 9, 4, 128), BF16),
            pltpu.VMEM((4, 9, 4, 128), BF16),
            pltpu.VMEM((8, 2, 128), BF16),
            pltpu.VMEM((4, 8, 2, 128), BF16),
            pltpu.VMEM((4, 4, 128), BF16),
            pltpu.VMEM((4, 4, 128), BF16),
            pltpu.VMEM((32, 2, 4, 128), BF16),
            pltpu.VMEM((2, 128), BF16),
            pltpu.VMEM((TERMS, 64, 2, 4, 128), BF16),
            pltpu.VMEM((TERMS, 64, 2, 128), BF16),
            pltpu.VMEM((TERMS, 64, 4, 128), BF16),
            pltpu.VMEM((2, 128), F32),
            pltpu.VMEM((2, states), BF16),
            pltpu.VMEM((TERMS, 2, 128), F32),
            pltpu.VMEM((TERMS, 2, states), BF16),
            pltpu.VMEM((2, channels), F32),
            pltpu.VMEM((TERMS, 16, 2, channels), F32),
            pltpu.VMEM((2, channels), F32),
            pltpu.VMEM((TERMS, 16, 2, channels), F32),
            pltpu.VMEM((TERMS, 2, channels), BF16),
            dma((9,)), dma((2,)), dma((2,)),
            dma, dma, dma, dma, dma, dma, dma, dma,
            dma, dma((TERMS,)), dma, dma((TERMS,)), dma, dma((TERMS,)),
            dma, dma((TERMS,)), dma, dma((TERMS,)), dma((16,)), dma((TERMS,)), dma((15,)),
        ],
        compiler_params=pltpu.CompilerParams(
            collective_id=0, has_side_effects=True, vmem_limit_bytes=60 * 1024 * 1024
        ),
    )(
        sizes, inner, ham, dip, amps.T, chan.reshape(1, channels), outer, energy, laser,
    )
    return pl.pallas_call(
        deliver,
        out_shape=(
            jax.ShapeDtypeStruct(inner.shape, F32),
            jax.ShapeDtypeStruct(outer.shape, F32),
        ),
        in_specs=[pl.BlockSpec(memory_space=pltpu.VMEM)] * 2,
        out_specs=(anywhere, anywhere),
        scratch_shapes=[dma((2,))],
        compiler_params=pltpu.CompilerParams(vmem_limit_bytes=1024 * 1024),
    )(*results)


def solution(mesh):
    placed = (
        P("sym", None, "dev"),
        P(),
        P("sym", "dev", None),
        P("sym", "dev", None),
        P(None, "dev"),
        P(),
        P(None, None, ("sym", "dev")),
        P(),
        P(),
    )
    return jax.shard_map(
        on_device,
        mesh=mesh,
        in_specs=placed,
        out_specs=(P("sym", None, "dev"), P(None, None, ("sym", "dev"))),
        check_vma=False,
    )
```

```python
import functools

import jax
import jax.numpy as jnp
from jax import lax
from jax.experimental import pallas as pl
from jax.experimental.pallas import tpu as pltpu
from jax.sharding import PartitionSpec as P

TERMS = 4
time_step = 0.012
spacing = 0.1
kinetic = 0.5 / (spacing * spacing)
block_scale = 90.0
dipole_scale = 40.0
laser_scale = 25.0

MESH = pl.DeviceIdType.MESH
F32, BF16 = jnp.float32, jnp.bfloat16
NT = (((1,), (1,)), ((), ()))

SYM, DEV = 4, 64
TOP = 8


def torus(step):
    return min(step, 4 - step)


OFFSETS = sorted(
    [(oy, ox) for oy in range(4) for ox in range(4) if (oy, ox) != (0, 0)],
    key=lambda o: -(torus(o[0]) + torus(o[1])),
)


def remote(src, dst, send, recv, sym, dev):
    return pltpu.make_async_remote_copy(
        src_ref=src, dst_ref=dst, send_sem=send, recv_sem=recv, device_id=(sym, dev), device_id_type=MESH
    )


def drain(ref, sem):
    pltpu.make_async_copy(ref, ref, sem).wait()


def kernel(
    sizes_in, inner, ham, dip, amps, chan, outer, energy, laser,
    inner_out, outer_out,
    sizes, inn, mats, dips, ampv, chv, out_raw, env, lasv, u, acc, wsum,
    stage1, got1, stage2, own, stage3, above, stage4, below,
    staged, first2, got, above_d, below_d, lows, highs, lower_h, upper_h,
    bst, bgot, bst2, bgot2, sgot,
    load, halo_send, halo_recv, send1, recv1, send2, recv2, send3, recv3, send4, recv4,
    sendd, recvd, sendx, recvx, sendh, recvh,
    bsend, brecv, bsend2, brecv2, ssend, srecv, ssend2,
):
    s = lax.axis_index("sym")
    d = lax.axis_index("dev")
    y, zl, x = d // 16, (d // 4) % 4, d % 4
    plane = y * 4 + x
    parity = x % 2
    group = s * 4 + zl
    is_plane_root = plane == 0
    is_root = jnp.logical_and(s == 0, d == 0)
    is_last = jnp.logical_and(s == SYM - 1, d == DEV - 1)
    channels = ampv.shape[1]
    points = out_raw.shape[2]
    rows = u.shape[1]

    def dev_of(y_, z_, x_):
        return (y_ * 4 + z_) * 4 + x_

    barrier = pltpu.get_barrier_semaphore()

    def greet(sym, dev):
        pl.semaphore_signal(barrier, inc=1, device_id=(sym, dev), device_id_type=MESH)

    for oy, ox in OFFSETS:
        greet(s, dev_of((y + oy) % 4, zl, (x + ox) % 4))
    for oz in range(1, 4):
        greet(s, dev_of(y, (zl + oz) % 4, x))
    expected = jnp.int32(18)
    has_below = s > 0
    has_above = s < SYM - 1

    @pl.when(has_below)
    def _():
        for z_ in range(4):
            greet(s - 1, dev_of(y, z_, x))

    @pl.when(has_above)
    def _():
        for z_ in range(4):
            greet(s + 1, dev_of(y, z_, x))

    expected += 4 * has_below.astype(jnp.int32) + 4 * has_above.astype(jnp.int32)

    @pl.when(is_root)
    def _():
        for g in range(1, 16):
            greet(jnp.int32(g // 4), jnp.int32((g % 4) * 4))

    hears_root = jnp.logical_and(is_plane_root, jnp.logical_not(is_root))

    @pl.when(hears_root)
    def _():
        greet(jnp.int32(0), jnp.int32(0))

    expected += 15 * is_root.astype(jnp.int32) + hears_root.astype(jnp.int32)
    position = s * DEV + d
    left, right = position - 1, position + 1
    has_left = jnp.logical_not(is_root)
    has_right = jnp.logical_not(is_last)

    @pl.when(has_left)
    def _():
        greet(left // DEV, left % DEV)

    @pl.when(has_right)
    def _():
        greet(right // DEV, right % DEV)

    expected += has_left.astype(jnp.int32) + has_right.astype(jnp.int32)

    pairs = (
        (sizes_in, sizes), (inner, inn), (dip, dips), (amps, ampv), (chan, chv),
        (outer, out_raw), (energy, env), (laser, lasv), (ham, mats),
    )
    loads = [pltpu.make_async_copy(src, dst, load.at[n]) for n, (src, dst) in enumerate(pairs)]
    for one in loads:
        one.start()

    for one in loads[0:3]:
        one.wait()
    size0, size1 = sizes[2 * s], sizes[2 * s + 1]
    row_index = d * 64 + lax.broadcasted_iota(jnp.int32, (2, 64), 1)
    live0 = row_index < size0
    live1 = row_index < size1
    zero2 = jnp.zeros((2, 64), BF16)
    zero4 = jnp.zeros((4, 64), BF16)

    def products(state):
        half = state.astype(BF16)
        spread = jnp.concatenate(
            [jnp.concatenate([half[0:2], zero2], axis=1), jnp.concatenate([zero2, half[2:4]], axis=1)], axis=0
        )
        flat = dips[...].reshape(128, dips.shape[2])
        part = jnp.dot(spread, flat, preferred_element_type=F32).astype(BF16)
        even = jnp.concatenate([half, zero4], axis=1)
        odd = jnp.concatenate([zero4, half], axis=1)
        chunk = jnp.where(parity == 0, even, odd)
        return chunk, part

    def stage_boundary(state):
        per_block = jnp.dot(state.astype(BF16), ampv[...], preferred_element_type=F32)
        bst[...] = owned0 * per_block[0:2] + owned1 * per_block[2:4]

    def prepare_plane(state):
        chunk, part = products(state)
        for y_ in range(4):
            for xh in range(2):
                stage1[y_ * 2 + xh, 0] = chunk
                for z_ in range(4):
                    tile = (y_ * 4 + z_) * 2 + xh
                    stage1[y_ * 2 + xh, 1 + z_] = part[:, tile * 128 : (tile + 1) * 128]

    def prepare_direct(state):
        chunk, part = products(state)
        first2[...] = chunk[0:2]
        for tile in range(32):
            staged[tile, 0] = chunk
            staged[tile, 1] = part[:, tile * 128 : (tile + 1) * 128]

    first = jnp.concatenate(
        [jnp.where(live0, inn[0], 0.0), jnp.where(live1, inn[1], 0.0)], axis=0
    )
    wsum[...] = first
    loads[3].wait()
    loads[4].wait()
    owned0 = (chv[...] == 2 * s).astype(F32)
    owned1 = (chv[...] == 2 * s + 1).astype(F32)
    prepare_plane(first)
    stage_boundary(first)

    loads[5].wait()
    blank = jnp.zeros((2, TOP, channels), F32)

    @pl.when(is_root)
    def _():
        u[:, 0:TOP, :] = blank

    @pl.when(is_last)
    def _():
        u[:, TOP + points : rows, :] = blank

    for i in range(2):
        turned = jnp.transpose(out_raw[i])
        u[i, TOP : TOP + points, :] = turned
        acc[i] = turned

    def slope_of(i):
        near = u[i, TOP : TOP + 8, :]
        return (-3.0 * near[0:1] + 4.0 * near[1:2] - near[2:3]) * (0.5 / spacing)

    def stage_slope(k):
        both = jnp.concatenate([slope_of(0), slope_of(1)], axis=0)
        sgot[k] = both.astype(BF16)

    @pl.when(is_root)
    def _():
        stage_slope(0)

    for one in loads[6:9]:
        one.wait()
    line = lax.broadcasted_iota(jnp.int32, (rows, 1), 0)
    inside = jnp.logical_and(
        jnp.logical_or(line >= TOP, has_left), jnp.logical_or(line < TOP + points, has_right)
    )

    to_left = remote(
        u.at[:, pl.ds(TOP, 8), :], u.at[:, pl.ds(TOP + points, 8), :],
        halo_send.at[0], halo_recv.at[0], left // DEV, left % DEV,
    )
    to_right = remote(
        u.at[:, pl.ds(points, 8), :], u.at[:, pl.ds(0, 8), :],
        halo_send.at[1], halo_recv.at[1], right // DEV, right % DEV,
    )

    def slope_to(k, g):
        return remote(
            sgot.at[k], sgot.at[k], ssend.at[g], srecv.at[k], jnp.int32(g // 4), jnp.int32((g % 4) * 4)
        )

    def slope_on(k, n):
        oy, ox = OFFSETS[n]
        return remote(sgot.at[k], sgot.at[k], ssend2.at[n], srecv.at[k], s, dev_of(oy, zl, ox))

    def factor_of(k):
        return time_step / (k + 1) if isinstance(k, int) else time_step / (k + 1).astype(F32)

    def close_grid(k):
        drain(bgot2.at[k, pl.ds(0, 15)], brecv2.at[k])
        edge = jnp.sum(bgot2[k], axis=0) * (-kinetic * factor_of(k))
        u[0, TOP : TOP + 1, :] += edge[1:2]
        u[1, TOP : TOP + 1, :] -= edge[0:1]
        acc[0, 0:1, :] += edge[1:2]
        acc[1, 0:1, :] -= edge[0:1]

    def send_boundary(k):
        @pl.when(is_plane_root)
        def _():
            bgot[k, 0] = bst[...]

        @pl.when(jnp.logical_not(is_plane_root))
        def _():
            remote(bst, bgot.at[k, plane], bsend, brecv.at[k], s, dev_of(0, zl, 0)).start()

    def send_slope(k):
        for g in range(1, 16):
            slope_to(k, g).start()

    def relay(k):
        @pl.when(hears_root)
        def _():
            drain(sgot.at[k], srecv.at[k])

        for n in range(15):
            slope_on(k, n).start()
        drain(bgot.at[k, pl.ds(0, 15)], brecv.at[k])
        total = jnp.sum(bgot[k], axis=0)

        @pl.when(is_root)
        def _():
            bgot2[k, 0] = total

        @pl.when(hears_root)
        def _():
            bst2[...] = total
            remote(bst2, bgot2.at[k, group], bsend2, brecv2.at[k], jnp.int32(0), jnp.int32(0)).start()

    def outer_update(k):
        factor = factor_of(k)
        images = []
        levels = env[...].reshape(1, channels)
        for i in range(2):
            value = u[i]
            mixed = jnp.dot(value.astype(BF16), lasv[...], preferred_element_type=F32)
            curve = pltpu.roll(value, 1, 0) - 2.0 * value + pltpu.roll(value, rows - 1, 0)
            image = -kinetic * curve + levels * value + laser_scale * mixed
            images.append(jnp.where(inside, image, 0.0))
        new0 = factor * images[1]
        new1 = -factor * images[0]
        u[0] = new0
        u[1] = new1
        acc[0] += new0[TOP : TOP + points]
        acc[1] += new1[TOP : TOP + points]

    def times(vectors, matrix):
        return lax.dot_general(vectors, matrix, NT, preferred_element_type=F32)

    def half_of(tile):
        return jnp.where(parity == 0, tile[:, 0:64], tile[:, 64:128])

    def slope_term(k):
        @pl.when(jnp.logical_not(is_plane_root))
        def _():
            drain(sgot.at[k], srecv.at[k])

        slope = sgot[k].astype(F32)
        masked = jnp.concatenate([owned0 * slope, owned1 * slope], axis=0).astype(BF16)
        return lax.dot_general(masked, ampv[...], NT, preferred_element_type=F32)

    def next_slope(k):
        close_grid(k)
        stage_slope(k + 1)
        send_slope(k + 1)

    def finish(k, image0, image1):
        image0 = jnp.where(live0, image0, 0.0)
        image1 = jnp.where(live1, image1, 0.0)
        fresh = factor_of(k) * jnp.concatenate(
            [image0[1:2], -image0[0:1], image1[1:2], -image1[0:1]], axis=0
        )
        wsum[...] += fresh

        @pl.when(jnp.logical_not(is_plane_root))
        def _():
            drain(bst, bsend)

        def ahead():
            stage_boundary(fresh)
            send_boundary(k + 1)

        if isinstance(k, int):
            ahead()
        else:
            pl.when(k < TERMS - 1)(ahead)
        return fresh

    def sent_slope(k):
        @pl.when(is_plane_root)
        def _():
            for n in range(15):
                slope_on(k, n).wait_send()

        @pl.when(is_root)
        def _():
            for g in range(1, 16):
                slope_to(k, g).wait_send()

        @pl.when(hears_root)
        def _():
            drain(bst2, bsend2)

    pl.semaphore_wait(barrier, expected)

    send_boundary(0)
    for n, (oy, ox) in enumerate(OFFSETS):
        ty, tx = (y + oy) % 4, (x + ox) % 4
        remote(
            stage1.at[ty * 2 + tx // 2], got1.at[plane], send1, recv1, s, dev_of(ty, zl, tx)
        ).start()

    @pl.when(is_root)
    def _():
        send_slope(0)

    @pl.when(has_left)
    def _():
        to_left.start()

    @pl.when(has_right)
    def _():
        to_right.start()

    got1[plane] = stage1[y * 2 + x // 2]
    drain(got1.at[pl.ds(0, 15)], recv1)

    sums = got1[0, 1:5].astype(F32)
    for p in range(1, 16):
        sums += got1[p, 1:5].astype(F32)
    sums = sums.astype(BF16)
    tiles = [got1[2 * q, 0] + got1[2 * q + 1, 0] for q in range(8)]
    for z_ in range(4):
        for q in range(8):
            stage2[z_, q] = tiles[q]
        stage2[z_, 8] = sums[z_]
        stage4[z_] = sums[z_]
    for q in range(8):
        stage3[q] = tiles[q][0:2]

    @pl.when(has_below)
    def _():
        for z_ in range(4):
            remote(stage3, above.at[zl], send3, recv3, s - 1, dev_of(y, z_, x)).start()

    @pl.when(has_above)
    def _():
        for z_ in range(4):
            remote(stage4.at[z_], below.at[zl], send4, recv4, s + 1, dev_of(y, z_, x)).start()

    for oz in (2, 1, 3):
        tz = (zl + oz) % 4
        remote(stage2.at[tz], own.at[zl], send2, recv2, s, dev_of(y, tz, x)).start()
    own[zl] = stage2[zl]

    @pl.when(is_plane_root)
    def _():
        relay(0)

    @pl.when(has_left)
    def _():
        to_right.wait_recv()
        to_left.wait_send()

    @pl.when(has_right)
    def _():
        to_left.wait_recv()
        to_right.wait_send()

    outer_update(0)

    drain(own.at[pl.ds(0, 3)], recv2)

    @pl.when(has_above)
    def _():
        drain(above, recv3)

    @pl.when(has_below)
    def _():
        drain(below, recv4)

    order = [(y_, z_, xh) for y_ in range(4) for z_ in range(4) for xh in range(2)]
    mine = jnp.concatenate([own[z_, y_ * 2 + xh] for y_, z_, xh in order], axis=1)
    upper = jnp.concatenate([above[z_, y_ * 2 + xh] for y_, z_, xh in order], axis=1)
    lower0 = below[0].astype(F32)
    lower1 = own[0, 8].astype(F32)
    for z_ in range(1, 4):
        lower0 += below[z_].astype(F32)
        lower1 += own[z_, 8].astype(F32)
    lower0 = jnp.where(has_below, half_of(lower0)[2:4], 0.0)
    lower1 = half_of(lower1)[0:2]
    forward1 = jnp.where(has_above, times(upper, dips[1]), 0.0)
    image0 = block_scale * times(mine, mats[0])[0:2] + dipole_scale * (times(mine, dips[0])[2:4] + lower0)
    image1 = block_scale * times(mine, mats[1])[2:4] + dipole_scale * (forward1 + lower1)
    bloch = slope_term(0)
    fresh = finish(0, image0 + bloch[0:2], image1 + bloch[2:4])

    @pl.when(is_root)
    def _():
        next_slope(0)

    prepare_direct(fresh)
    drain(got1.at[pl.ds(0, 15)], send1)
    drain(own.at[pl.ds(0, 3)], send2)

    @pl.when(has_below)
    def _():
        drain(above, send3)

    @pl.when(has_above)
    def _():
        drain(below, send4)

    sent_slope(0)
    partner = s + 1 - 2 * (s % 2)
    is_low = s % 2 == 0
    is_high = s % 2 == 1

    @pl.loop(1, TERMS)
    def _(k):
        for level in range(4, -1, -1):
            ring = [o for o in OFFSETS + [(0, 0)] if torus(o[0]) + torus(o[1]) == level]
            targets = [
                (dev_of((y + oy) % 4, (zl + oz) % 4, (x + ox) % 4), (oy, oz, ox)) for oz in (2, 1, 3, 0) for oy, ox in ring
            ]

            @pl.when(s == 1)
            def _():
                for to, _o in targets:
                    remote(staged.at[to // 2, 1], below_d.at[k, d], sendx, recvx.at[k], jnp.int32(2), to).start()

            @pl.when(s == 2)
            def _():
                for to, _o in targets:
                    remote(first2, above_d.at[k, d], sendx, recvx.at[k], jnp.int32(1), to).start()

            for to, offset in targets:
                if offset != (0, 0, 0):
                    remote(staged.at[to // 2], got.at[k, d], sendd, recvd.at[k], s, to).start()

        got[k, d] = staged[d // 2]

        @pl.when(is_plane_root)
        def _():
            relay(k)

        outer_update(k)

        @pl.when(jnp.logical_and(k == TERMS - 1, jnp.logical_not(is_root)))
        def _():
            for i in range(2):
                outer_out[i] = jnp.transpose(acc[i])

        drain(got.at[k, pl.ds(0, 63)], recvd.at[k])
        give_low = remote(lows, lower_h.at[k], sendh, recvh.at[k], partner, d)
        give_high = remote(highs, upper_h.at[k], sendh, recvh.at[k], partner, d)

        @pl.when(is_high)
        def _():
            for q in range(32):
                highs[:, q * 128 : (q + 1) * 128] = got[k, 2 * q, 0, 0:2] + got[k, 2 * q + 1, 0, 0:2]
            give_high.start()

        sums = got[k, 0, 1].astype(F32)
        for p in range(1, 64):
            sums += got[k, p, 1].astype(F32)

        @pl.when(is_low)
        def _():
            lows[...] = sums[2:4]
            give_low.start()

        mine = jnp.concatenate([got[k, 2 * q, 0] + got[k, 2 * q + 1, 0] for q in range(32)], axis=1)
        image0 = block_scale * times(mine, mats[0])[0:2] + dipole_scale * times(mine, dips[0])[2:4]
        image1 = block_scale * times(mine, mats[1])[2:4] + dipole_scale * half_of(sums)[0:2]
        bloch = slope_term(k)
        image0 += bloch[0:2]
        image1 += bloch[2:4]

        @pl.when(jnp.logical_and(is_root, k < TERMS - 1))
        def _():
            next_slope(k)

        @pl.when(s == 1)
        def _():
            drain(above_d.at[k], recvx.at[k])
            for q in range(32):
                upper_h[k, :, q * 128 : (q + 1) * 128] = above_d[k, 2 * q] + above_d[k, 2 * q + 1]

        @pl.when(s == 2)
        def _():
            drain(below_d.at[k], recvx.at[k])
            total = below_d[k, 0].astype(F32)
            for p in range(1, 64):
                total += below_d[k, p].astype(F32)
            lower_h[k] = total[2:4]

        @pl.when(is_low)
        def _():
            drain(upper_h.at[k], recvh.at[k])

        @pl.when(is_high)
        def _():
            drain(lower_h.at[k], recvh.at[k])

        image0 += jnp.where(has_below, dipole_scale * half_of(lower_h[k]), 0.0)
        image1 += jnp.where(has_above, dipole_scale * times(upper_h[k], dips[1]), 0.0)
        fresh = finish(k, image0, image1)

        drain(got.at[k, pl.ds(0, 63)], sendd)

        @pl.when(s == 1)
        def _():
            drain(below_d.at[k], sendx)

        @pl.when(s == 2)
        def _():
            drain(above_d.at[k], sendx)

        @pl.when(k < TERMS - 1)
        def _():
            prepare_direct(fresh)

        @pl.when(is_low)
        def _():
            drain(lower_h.at[k], sendh)

        @pl.when(is_high)
        def _():
            drain(upper_h.at[k], sendh)

        sent_slope(k)

    inner_out[0] = wsum[0:2]
    inner_out[1] = wsum[2:4]

    @pl.when(is_root)
    def _():
        close_grid(TERMS - 1)
        for i in range(2):
            outer_out[i] = jnp.transpose(acc[i])


def deliver(inner_v, outer_v, inner_out, outer_out, sems):
    copies = [
        pltpu.make_async_copy(outer_v, outer_out, sems.at[0]),
        pltpu.make_async_copy(inner_v, inner_out, sems.at[1]),
    ]
    for one in copies:
        one.start()
    for one in copies:
        one.wait()


def on_device(inner, sizes, ham, dip, amps, chan, outer, energy, laser):
    blocks, parts, own_rows = inner.shape
    states = ham.shape[2]
    channels, points = outer.shape[1], outer.shape[2]
    rows = points + 16
    dma = pltpu.SemaphoreType.DMA
    anywhere = pl.BlockSpec(memory_space=pl.ANY)
    results = pl.pallas_call(
        kernel,
        out_shape=(
            pltpu.VMEM(inner.shape, F32),
            pltpu.VMEM(outer.shape, F32),
        ),
        in_specs=[anywhere] * 9,
        out_specs=(pl.BlockSpec(memory_space=pltpu.VMEM), pl.BlockSpec(memory_space=pltpu.VMEM)),
        scratch_shapes=[
            pltpu.SMEM(sizes.shape, jnp.int32),
            pltpu.VMEM(inner.shape, F32),
            pltpu.VMEM(ham.shape, BF16),
            pltpu.VMEM(dip.shape, BF16),
            pltpu.VMEM((own_rows, channels), BF16),
            pltpu.VMEM((1, channels), jnp.int32),
            pltpu.VMEM(outer.shape, F32),
            pltpu.VMEM((channels,), F32),
            pltpu.VMEM(laser.shape, BF16),
            pltpu.VMEM((2, rows, channels), F32),
            pltpu.VMEM((2, points, channels), F32),
            pltpu.VMEM((4, own_rows), F32),
            pltpu.VMEM((8, 5, 4, 128), BF16),
            pltpu.VMEM((16, 5, 4, 128), BF16),
            pltpu.VMEM((4, 9, 4, 128), BF16),
            pltpu.VMEM((4, 9, 4, 128), BF16),
            pltpu.VMEM((8, 2, 128), BF16),
            pltpu.VMEM((4, 8, 2, 128), BF16),
            pltpu.VMEM((4, 4, 128), BF16),
            pltpu.VMEM((4, 4, 128), BF16),
            pltpu.VMEM((32, 2, 4, 128), BF16),
            pltpu.VMEM((2, 128), BF16),
            pltpu.VMEM((TERMS, 64, 2, 4, 128), BF16),
            pltpu.VMEM((TERMS, 64, 2, 128), BF16),
            pltpu.VMEM((TERMS, 64, 4, 128), BF16),
            pltpu.VMEM((2, 128), F32),
            pltpu.VMEM((2, states), BF16),
            pltpu.VMEM((TERMS, 2, 128), F32),
            pltpu.VMEM((TERMS, 2, states), BF16),
            pltpu.VMEM((2, channels), F32),
            pltpu.VMEM((TERMS, 16, 2, channels), F32),
            pltpu.VMEM((2, channels), F32),
            pltpu.VMEM((TERMS, 16, 2, channels), F32),
            pltpu.VMEM((TERMS, 2, channels), BF16),
            dma((9,)), dma((2,)), dma((2,)),
            dma, dma, dma, dma, dma, dma, dma, dma,
            dma, dma((TERMS,)), dma, dma((TERMS,)), dma, dma((TERMS,)),
            dma, dma((TERMS,)), dma, dma((TERMS,)), dma((16,)), dma((TERMS,)), dma((15,)),
        ],
        compiler_params=pltpu.CompilerParams(
            collective_id=0, has_side_effects=True, vmem_limit_bytes=60 * 1024 * 1024
        ),
    )(
        sizes, inner, ham, dip, amps.T, chan.reshape(1, channels), outer, energy, laser,
    )
    return pl.pallas_call(
        deliver,
        out_shape=(
            jax.ShapeDtypeStruct(inner.shape, F32),
            jax.ShapeDtypeStruct(outer.shape, F32),
        ),
        in_specs=[pl.BlockSpec(memory_space=pltpu.VMEM)] * 2,
        out_specs=(anywhere, anywhere),
        scratch_shapes=[dma((2,))],
        compiler_params=pltpu.CompilerParams(vmem_limit_bytes=1024 * 1024),
    )(*results)


def solution(mesh):
    placed = (
        P("sym", None, "dev"),
        P(),
        P("sym", "dev", None),
        P("sym", "dev", None),
        P(None, "dev"),
        P(),
        P(None, None, ("sym", "dev")),
        P(),
        P(),
    )
    return jax.shard_map(
        on_device,
        mesh=mesh,
        in_specs=placed,
        out_specs=(P("sym", None, "dev"), P(None, None, ("sym", "dev"))),
        check_vma=False,
    )
```

```python
import functools

import jax
import jax.numpy as jnp
from jax import lax
from jax.experimental import pallas as pl
from jax.experimental.pallas import tpu as pltpu
from jax.sharding import PartitionSpec as P

TERMS = 4
time_step = 0.012
spacing = 0.1
kinetic = 0.5 / (spacing * spacing)
block_scale = 90.0
dipole_scale = 40.0
laser_scale = 25.0

MESH = pl.DeviceIdType.MESH
F32, BF16 = jnp.float32, jnp.bfloat16
NT = (((1,), (1,)), ((), ()))

SYM, DEV = 4, 64
TOP = 8


def torus(step):
    return min(step, 4 - step)


OFFSETS = sorted(
    [(oy, ox) for oy in range(4) for ox in range(4) if (oy, ox) != (0, 0)],
    key=lambda o: -(torus(o[0]) + torus(o[1])),
)


def remote(src, dst, send, recv, sym, dev):
    return pltpu.make_async_remote_copy(
        src_ref=src, dst_ref=dst, send_sem=send, recv_sem=recv, device_id=(sym, dev), device_id_type=MESH
    )


def drain(ref, sem):
    pltpu.make_async_copy(ref, ref, sem).wait()


def kernel(
    sizes_in, inner, ham, dip, amps, chan, outer, energy, laser,
    inner_out, outer_out,
    sizes, inn, mats, dips, ampv, chv, out_raw, env, lasv, u, acc, wsum,
    stage1, got1, stage2, own, stage3, above, stage4, below,
    staged, first2, got, above_d, below_d, lows, highs, lower_h, upper_h,
    bst, bgot, bst2, bgot2, sgot,
    load, halo_send, halo_recv, send1, recv1, send2, recv2, send3, recv3, send4, recv4,
    sendd, recvd, sendx, recvx, sendh, recvh,
    bsend, brecv, bsend2, brecv2, ssend, srecv, ssend2,
):
    s = lax.axis_index("sym")
    d = lax.axis_index("dev")
    y, zl, x = d // 16, (d // 4) % 4, d % 4
    plane = y * 4 + x
    parity = x % 2
    group = s * 4 + zl
    is_plane_root = plane == 0
    is_root = jnp.logical_and(s == 0, d == 0)
    is_last = jnp.logical_and(s == SYM - 1, d == DEV - 1)
    channels = ampv.shape[1]
    points = out_raw.shape[2]
    rows = u.shape[1]

    def dev_of(y_, z_, x_):
        return (y_ * 4 + z_) * 4 + x_

    pairs = (
        (sizes_in, sizes), (inner, inn), (dip, dips), (amps, ampv), (chan, chv),
        (outer, out_raw), (energy, env), (laser, lasv), (ham, mats),
    )
    loads = [pltpu.make_async_copy(src, dst, load.at[n]) for n, (src, dst) in enumerate(pairs)]
    for one in loads[:3]:
        one.start()

    barrier = pltpu.get_barrier_semaphore()

    def greet(sym, dev):
        pl.semaphore_signal(barrier, inc=1, device_id=(sym, dev), device_id_type=MESH)

    for oy, ox in OFFSETS:
        greet(s, dev_of((y + oy) % 4, zl, (x + ox) % 4))
    for oz in range(1, 4):
        greet(s, dev_of(y, (zl + oz) % 4, x))
    expected = jnp.int32(18)
    has_below = s > 0
    has_above = s < SYM - 1

    @pl.when(has_below)
    def _():
        for z_ in range(4):
            greet(s - 1, dev_of(y, z_, x))

    @pl.when(has_above)
    def _():
        for z_ in range(4):
            greet(s + 1, dev_of(y, z_, x))

    expected += 4 * has_below.astype(jnp.int32) + 4 * has_above.astype(jnp.int32)

    @pl.when(is_root)
    def _():
        for g in range(1, 16):
            greet(jnp.int32(g // 4), jnp.int32((g % 4) * 4))

    hears_root = jnp.logical_and(is_plane_root, jnp.logical_not(is_root))

    @pl.when(hears_root)
    def _():
        greet(jnp.int32(0), jnp.int32(0))

    expected += 15 * is_root.astype(jnp.int32) + hears_root.astype(jnp.int32)
    position = s * DEV + d
    left, right = position - 1, position + 1
    has_left = jnp.logical_not(is_root)
    has_right = jnp.logical_not(is_last)

    @pl.when(has_left)
    def _():
        greet(left // DEV, left % DEV)

    @pl.when(has_right)
    def _():
        greet(right // DEV, right % DEV)

    expected += has_left.astype(jnp.int32) + has_right.astype(jnp.int32)

    for one in loads[3:]:
        one.start()

    for one in loads[0:3]:
        one.wait()
    size0, size1 = sizes[2 * s], sizes[2 * s + 1]
    row_index = d * 64 + lax.broadcasted_iota(jnp.int32, (2, 64), 1)
    live0 = row_index < size0
    live1 = row_index < size1
    zero2 = jnp.zeros((2, 64), BF16)
    zero4 = jnp.zeros((4, 64), BF16)

    def products(state):
        half = state.astype(BF16)
        spread = jnp.concatenate(
            [jnp.concatenate([half[0:2], zero2], axis=1), jnp.concatenate([zero2, half[2:4]], axis=1)], axis=0
        )
        flat = dips[...].reshape(128, dips.shape[2])
        part = jnp.dot(spread, flat, preferred_element_type=F32).astype(BF16)
        even = jnp.concatenate([half, zero4], axis=1)
        odd = jnp.concatenate([zero4, half], axis=1)
        chunk = jnp.where(parity == 0, even, odd)
        return chunk, part

    def stage_boundary(state):
        per_block = jnp.dot(state.astype(BF16), ampv[...], preferred_element_type=F32)
        bst[...] = owned0 * per_block[0:2] + owned1 * per_block[2:4]

    def prepare_plane(state):
        chunk, part = products(state)
        for y_ in range(4):
            for xh in range(2):
                stage1[y_ * 2 + xh, 0] = chunk
                for z_ in range(4):
                    tile = (y_ * 4 + z_) * 2 + xh
                    stage1[y_ * 2 + xh, 1 + z_] = part[:, tile * 128 : (tile + 1) * 128]

    def prepare_direct(state):
        chunk, part = products(state)
        first2[...] = chunk[0:2]
        for tile in range(32):
            staged[tile, 0] = chunk
            staged[tile, 1] = part[:, tile * 128 : (tile + 1) * 128]

    first = jnp.concatenate(
        [jnp.where(live0, inn[0], 0.0), jnp.where(live1, inn[1], 0.0)], axis=0
    )
    wsum[...] = first
    loads[3].wait()
    loads[4].wait()
    owned0 = (chv[...] == 2 * s).astype(F32)
    owned1 = (chv[...] == 2 * s + 1).astype(F32)
    prepare_plane(first)
    stage_boundary(first)

    def slope_of(i):
        near = u[i, TOP : TOP + 8, :]
        return (-3.0 * near[0:1] + 4.0 * near[1:2] - near[2:3]) * (0.5 / spacing)

    def stage_slope(k):
        both = jnp.concatenate([slope_of(0), slope_of(1)], axis=0)
        sgot[k] = both.astype(BF16)

    line = lax.broadcasted_iota(jnp.int32, (rows, 1), 0)
    inside = jnp.logical_and(
        jnp.logical_or(line >= TOP, has_left), jnp.logical_or(line < TOP + points, has_right)
    )

    to_left = remote(
        u.at[:, pl.ds(TOP, 8), :], u.at[:, pl.ds(TOP + points, 8), :],
        halo_send.at[0], halo_recv.at[0], left // DEV, left % DEV,
    )
    to_right = remote(
        u.at[:, pl.ds(points, 8), :], u.at[:, pl.ds(0, 8), :],
        halo_send.at[1], halo_recv.at[1], right // DEV, right % DEV,
    )

    def slope_to(k, g):
        return remote(
            sgot.at[k], sgot.at[k], ssend.at[g], srecv.at[k], jnp.int32(g // 4), jnp.int32((g % 4) * 4)
        )

    def slope_on(k, n):
        oy, ox = OFFSETS[n]
        return remote(sgot.at[k], sgot.at[k], ssend2.at[n], srecv.at[k], s, dev_of(oy, zl, ox))

    def factor_of(k):
        return time_step / (k + 1) if isinstance(k, int) else time_step / (k + 1).astype(F32)

    def edge_of(k):
        drain(bgot2.at[k, pl.ds(0, 15)], brecv2.at[k])
        edge = jnp.sum(bgot2[k], axis=0) * (-kinetic * factor_of(k))
        return edge[1:2], -edge[0:1]

    def send_boundary(k):
        @pl.when(is_plane_root)
        def _():
            bgot[k, 0] = bst[...]

        @pl.when(jnp.logical_not(is_plane_root))
        def _():
            remote(bst, bgot.at[k, plane], bsend, brecv.at[k], s, dev_of(0, zl, 0)).start()

    def send_slope(k):
        for g in range(1, 16):
            slope_to(k, g).start()

    def relay(k):
        @pl.when(hears_root)
        def _():
            drain(sgot.at[k], srecv.at[k])

        for n in range(15):
            slope_on(k, n).start()
        drain(bgot.at[k, pl.ds(0, 15)], brecv.at[k])
        total = jnp.sum(bgot[k], axis=0)

        @pl.when(is_root)
        def _():
            bgot2[k, 0] = total

        @pl.when(hears_root)
        def _():
            bst2[...] = total
            remote(bst2, bgot2.at[k, group], bsend2, brecv2.at[k], jnp.int32(0), jnp.int32(0)).start()

    def outer_update(k):
        factor = factor_of(k)
        images = []
        levels = env[...].reshape(1, channels)
        for i in range(2):
            value = u[i]
            mixed = jnp.dot(value.astype(BF16), lasv[...], preferred_element_type=F32)
            curve = pltpu.roll(value, 1, 0) - 2.0 * value + pltpu.roll(value, rows - 1, 0)
            image = -kinetic * curve + levels * value + laser_scale * mixed
            images.append(jnp.where(inside, image, 0.0))
        new0 = factor * images[1]
        new1 = -factor * images[0]
        u[0] = new0
        u[1] = new1
        acc[0] += new0[TOP : TOP + points]
        acc[1] += new1[TOP : TOP + points]

    def times(vectors, matrix):
        return lax.dot_general(vectors, matrix, NT, preferred_element_type=F32)

    def half_of(tile):
        return jnp.where(parity == 0, tile[:, 0:64], tile[:, 64:128])

    def slope_term(k):
        @pl.when(jnp.logical_not(is_plane_root))
        def _():
            drain(sgot.at[k], srecv.at[k])

        slope = sgot[k].astype(F32)
        masked = jnp.concatenate([owned0 * slope, owned1 * slope], axis=0).astype(BF16)
        return lax.dot_general(masked, ampv[...], NT, preferred_element_type=F32)

    def next_slope(k):
        fixes = edge_of(k)
        slopes = [slope_of(i) - (1.5 / spacing) * fixes[i] for i in range(2)]
        sgot[k + 1] = jnp.concatenate(slopes, axis=0).astype(BF16)
        send_slope(k + 1)
        for i in range(2):
            u[i, TOP : TOP + 1, :] += fixes[i]
            acc[i, 0:1, :] += fixes[i]

    def last_column(k):
        fixes = edge_of(k)
        columns = jnp.transpose(jnp.concatenate([*fixes, jnp.zeros((6, channels), F32)], axis=0))
        for i in range(2):
            outer_out[i, :, 0:1] += columns[:, i : i + 1]

    def finish(k, image0, image1):
        image0 = jnp.where(live0, image0, 0.0)
        image1 = jnp.where(live1, image1, 0.0)
        fresh = factor_of(k) * jnp.concatenate(
            [image0[1:2], -image0[0:1], image1[1:2], -image1[0:1]], axis=0
        )
        wsum[...] += fresh

        @pl.when(jnp.logical_not(is_plane_root))
        def _():
            drain(bst, bsend)

        def ahead():
            stage_boundary(fresh)
            send_boundary(k + 1)

        if isinstance(k, int):
            ahead()
        else:
            pl.when(k < TERMS - 1)(ahead)
        return fresh

    def sent_slope(k):
        @pl.when(is_plane_root)
        def _():
            for n in range(15):
                slope_on(k, n).wait_send()

        @pl.when(is_root)
        def _():
            for g in range(1, 16):
                slope_to(k, g).wait_send()

        @pl.when(hears_root)
        def _():
            drain(bst2, bsend2)

    pl.semaphore_wait(barrier, expected)

    send_boundary(0)
    for n, (oy, ox) in enumerate(OFFSETS):
        ty, tx = (y + oy) % 4, (x + ox) % 4
        remote(
            stage1.at[ty * 2 + tx // 2], got1.at[plane], send1, recv1, s, dev_of(ty, zl, tx)
        ).start()

    loads[5].wait()
    blank = jnp.zeros((2, TOP, channels), F32)

    @pl.when(is_root)
    def _():
        u[:, 0:TOP, :] = blank

    @pl.when(is_last)
    def _():
        u[:, TOP + points : rows, :] = blank

    for i in range(2):
        turned = jnp.transpose(out_raw[i])
        u[i, TOP : TOP + points, :] = turned
        acc[i] = turned

    @pl.when(is_root)
    def _():
        stage_slope(0)
        send_slope(0)

    @pl.when(has_left)
    def _():
        to_left.start()

    @pl.when(has_right)
    def _():
        to_right.start()

    for one in loads[6:9]:
        one.wait()
    got1[plane] = stage1[y * 2 + x // 2]
    drain(got1.at[pl.ds(0, 15)], recv1)

    sums = got1[0, 1:5].astype(F32)
    for p in range(1, 16):
        sums += got1[p, 1:5].astype(F32)
    sums = sums.astype(BF16)
    tiles = [got1[2 * q, 0] + got1[2 * q + 1, 0] for q in range(8)]
    for z_ in range(4):
        for q in range(8):
            stage2[z_, q] = tiles[q]
        stage2[z_, 8] = sums[z_]
        stage4[z_] = sums[z_]
    for q in range(8):
        stage3[q] = tiles[q][0:2]

    @pl.when(has_below)
    def _():
        for z_ in range(4):
            remote(stage3, above.at[zl], send3, recv3, s - 1, dev_of(y, z_, x)).start()

    @pl.when(has_above)
    def _():
        for z_ in range(4):
            remote(stage4.at[z_], below.at[zl], send4, recv4, s + 1, dev_of(y, z_, x)).start()

    for oz in (2, 1, 3):
        tz = (zl + oz) % 4
        remote(stage2.at[tz], own.at[zl], send2, recv2, s, dev_of(y, tz, x)).start()
    own[zl] = stage2[zl]

    @pl.when(is_plane_root)
    def _():
        relay(0)

    @pl.when(has_left)
    def _():
        to_right.wait_recv()
        to_left.wait_send()

    @pl.when(has_right)
    def _():
        to_left.wait_recv()
        to_right.wait_send()

    outer_update(0)

    drain(own.at[pl.ds(0, 3)], recv2)

    @pl.when(has_above)
    def _():
        drain(above, recv3)

    @pl.when(has_below)
    def _():
        drain(below, recv4)

    order = [(y_, z_, xh) for y_ in range(4) for z_ in range(4) for xh in range(2)]
    mine = jnp.concatenate([own[z_, y_ * 2 + xh] for y_, z_, xh in order], axis=1)
    upper = jnp.concatenate([above[z_, y_ * 2 + xh] for y_, z_, xh in order], axis=1)
    lower0 = below[0].astype(F32)
    lower1 = own[0, 8].astype(F32)
    for z_ in range(1, 4):
        lower0 += below[z_].astype(F32)
        lower1 += own[z_, 8].astype(F32)
    lower0 = jnp.where(has_below, half_of(lower0)[2:4], 0.0)
    lower1 = half_of(lower1)[0:2]
    forward1 = jnp.where(has_above, times(upper, dips[1]), 0.0)
    image0 = block_scale * times(mine, mats[0])[0:2] + dipole_scale * (times(mine, dips[0])[2:4] + lower0)
    image1 = block_scale * times(mine, mats[1])[2:4] + dipole_scale * (forward1 + lower1)
    bloch = slope_term(0)
    fresh = finish(0, image0 + bloch[0:2], image1 + bloch[2:4])

    @pl.when(is_root)
    def _():
        next_slope(0)

    prepare_direct(fresh)
    drain(got1.at[pl.ds(0, 15)], send1)
    drain(own.at[pl.ds(0, 3)], send2)

    @pl.when(has_below)
    def _():
        drain(above, send3)

    @pl.when(has_above)
    def _():
        drain(below, send4)

    sent_slope(0)
    partner = s + 1 - 2 * (s % 2)
    is_low = s % 2 == 0
    is_high = s % 2 == 1

    @pl.loop(1, TERMS)
    def _(k):
        for level in range(4, -1, -1):
            ring = [o for o in OFFSETS + [(0, 0)] if torus(o[0]) + torus(o[1]) == level]
            targets = [
                (dev_of((y + oy) % 4, (zl + oz) % 4, (x + ox) % 4), (oy, oz, ox)) for oz in (2, 1, 3, 0) for oy, ox in ring
            ]

            @pl.when(s == 1)
            def _():
                for to, _o in targets:
                    remote(staged.at[to // 2, 1], below_d.at[k, d], sendx, recvx.at[k], jnp.int32(2), to).start()

            @pl.when(s == 2)
            def _():
                for to, _o in targets:
                    remote(first2, above_d.at[k, d], sendx, recvx.at[k], jnp.int32(1), to).start()

            for to, offset in targets:
                if offset != (0, 0, 0):
                    remote(staged.at[to // 2], got.at[k, d], sendd, recvd.at[k], s, to).start()

        got[k, d] = staged[d // 2]

        @pl.when(is_plane_root)
        def _():
            relay(k)

        outer_update(k)

        @pl.when(k == TERMS - 1)
        def _():
            for i in range(2):
                outer_out[i] = jnp.transpose(acc[i])

        drain(got.at[k, pl.ds(0, 63)], recvd.at[k])
        give_low = remote(lows, lower_h.at[k], sendh, recvh.at[k], partner, d)
        give_high = remote(highs, upper_h.at[k], sendh, recvh.at[k], partner, d)

        @pl.when(is_high)
        def _():
            for q in range(32):
                highs[:, q * 128 : (q + 1) * 128] = got[k, 2 * q, 0, 0:2] + got[k, 2 * q + 1, 0, 0:2]
            give_high.start()

        sums = got[k, 0, 1].astype(F32)
        for p in range(1, 64):
            sums += got[k, p, 1].astype(F32)

        @pl.when(is_low)
        def _():
            lows[...] = sums[2:4]
            give_low.start()

        mine = jnp.concatenate([got[k, 2 * q, 0] + got[k, 2 * q + 1, 0] for q in range(32)], axis=1)
        image0 = block_scale * times(mine, mats[0])[0:2] + dipole_scale * times(mine, dips[0])[2:4]
        image1 = block_scale * times(mine, mats[1])[2:4] + dipole_scale * half_of(sums)[0:2]
        bloch = slope_term(k)
        image0 += bloch[0:2]
        image1 += bloch[2:4]

        @pl.when(jnp.logical_and(is_root, k < TERMS - 1))
        def _():
            next_slope(k)

        @pl.when(jnp.logical_and(is_root, k == TERMS - 1))
        def _():
            last_column(k)

        @pl.when(s == 1)
        def _():
            drain(above_d.at[k], recvx.at[k])
            for q in range(32):
                upper_h[k, :, q * 128 : (q + 1) * 128] = above_d[k, 2 * q] + above_d[k, 2 * q + 1]

        @pl.when(s == 2)
        def _():
            drain(below_d.at[k], recvx.at[k])
            total = below_d[k, 0].astype(F32)
            for p in range(1, 64):
                total += below_d[k, p].astype(F32)
            lower_h[k] = total[2:4]

        @pl.when(is_low)
        def _():
            drain(upper_h.at[k], recvh.at[k])

        @pl.when(is_high)
        def _():
            drain(lower_h.at[k], recvh.at[k])

        image0 += jnp.where(has_below, dipole_scale * half_of(lower_h[k]), 0.0)
        image1 += jnp.where(has_above, dipole_scale * times(upper_h[k], dips[1]), 0.0)
        fresh = finish(k, image0, image1)

        drain(got.at[k, pl.ds(0, 63)], sendd)

        @pl.when(s == 1)
        def _():
            drain(below_d.at[k], sendx)

        @pl.when(s == 2)
        def _():
            drain(above_d.at[k], sendx)

        @pl.when(k < TERMS - 1)
        def _():
            prepare_direct(fresh)

        @pl.when(is_low)
        def _():
            drain(lower_h.at[k], sendh)

        @pl.when(is_high)
        def _():
            drain(upper_h.at[k], sendh)

        sent_slope(k)

    inner_out[0] = wsum[0:2]
    inner_out[1] = wsum[2:4]


def deliver(inner_v, outer_v, inner_out, outer_out, sems):
    copies = [
        pltpu.make_async_copy(outer_v, outer_out, sems.at[0]),
        pltpu.make_async_copy(inner_v, inner_out, sems.at[1]),
    ]
    for one in copies:
        one.start()
    for one in copies:
        one.wait()


def on_device(inner, sizes, ham, dip, amps, chan, outer, energy, laser):
    blocks, parts, own_rows = inner.shape
    states = ham.shape[2]
    channels, points = outer.shape[1], outer.shape[2]
    rows = points + 16
    dma = pltpu.SemaphoreType.DMA
    anywhere = pl.BlockSpec(memory_space=pl.ANY)
    results = pl.pallas_call(
        kernel,
        out_shape=(
            pltpu.VMEM(inner.shape, F32),
            pltpu.VMEM(outer.shape, F32),
        ),
        in_specs=[anywhere] * 9,
        out_specs=(pl.BlockSpec(memory_space=pltpu.VMEM), pl.BlockSpec(memory_space=pltpu.VMEM)),
        scratch_shapes=[
            pltpu.SMEM(sizes.shape, jnp.int32),
            pltpu.VMEM(inner.shape, F32),
            pltpu.VMEM(ham.shape, BF16),
            pltpu.VMEM(dip.shape, BF16),
            pltpu.VMEM((own_rows, channels), BF16),
            pltpu.VMEM((1, channels), jnp.int32),
            pltpu.VMEM(outer.shape, F32),
            pltpu.VMEM((channels,), F32),
            pltpu.VMEM(laser.shape, BF16),
            pltpu.VMEM((2, rows, channels), F32),
            pltpu.VMEM((2, points, channels), F32),
            pltpu.VMEM((4, own_rows), F32),
            pltpu.VMEM((8, 5, 4, 128), BF16),
            pltpu.VMEM((16, 5, 4, 128), BF16),
            pltpu.VMEM((4, 9, 4, 128), BF16),
            pltpu.VMEM((4, 9, 4, 128), BF16),
            pltpu.VMEM((8, 2, 128), BF16),
            pltpu.VMEM((4, 8, 2, 128), BF16),
            pltpu.VMEM((4, 4, 128), BF16),
            pltpu.VMEM((4, 4, 128), BF16),
            pltpu.VMEM((32, 2, 4, 128), BF16),
            pltpu.VMEM((2, 128), BF16),
            pltpu.VMEM((TERMS, 64, 2, 4, 128), BF16),
            pltpu.VMEM((TERMS, 64, 2, 128), BF16),
            pltpu.VMEM((TERMS, 64, 4, 128), BF16),
            pltpu.VMEM((2, 128), F32),
            pltpu.VMEM((2, states), BF16),
            pltpu.VMEM((TERMS, 2, 128), F32),
            pltpu.VMEM((TERMS, 2, states), BF16),
            pltpu.VMEM((2, channels), F32),
            pltpu.VMEM((TERMS, 16, 2, channels), F32),
            pltpu.VMEM((2, channels), F32),
            pltpu.VMEM((TERMS, 16, 2, channels), F32),
            pltpu.VMEM((TERMS, 2, channels), BF16),
            dma((9,)), dma((2,)), dma((2,)),
            dma, dma, dma, dma, dma, dma, dma, dma,
            dma, dma((TERMS,)), dma, dma((TERMS,)), dma, dma((TERMS,)),
            dma, dma((TERMS,)), dma, dma((TERMS,)), dma((16,)), dma((TERMS,)), dma((15,)),
        ],
        compiler_params=pltpu.CompilerParams(
            collective_id=0, has_side_effects=True, vmem_limit_bytes=60 * 1024 * 1024
        ),
    )(
        sizes, inner, ham, dip, amps.T, chan.reshape(1, channels), outer, energy, laser,
    )
    return pl.pallas_call(
        deliver,
        out_shape=(
            jax.ShapeDtypeStruct(inner.shape, F32),
            jax.ShapeDtypeStruct(outer.shape, F32),
        ),
        in_specs=[pl.BlockSpec(memory_space=pltpu.VMEM)] * 2,
        out_specs=(anywhere, anywhere),
        scratch_shapes=[dma((2,))],
        compiler_params=pltpu.CompilerParams(vmem_limit_bytes=1024 * 1024),
    )(*results)


def solution(mesh):
    placed = (
        P("sym", None, "dev"),
        P(),
        P("sym", "dev", None),
        P("sym", "dev", None),
        P(None, "dev"),
        P(),
        P(None, None, ("sym", "dev")),
        P(),
        P(),
    )
    return jax.shard_map(
        on_device,
        mesh=mesh,
        in_specs=placed,
        out_specs=(P("sym", None, "dev"), P(None, None, ("sym", "dev"))),
        check_vma=False,
    )
```

```python
import functools

import jax
import jax.numpy as jnp
from jax import lax
from jax.experimental import pallas as pl
from jax.experimental.pallas import tpu as pltpu
from jax.sharding import PartitionSpec as P

TERMS = 4
time_step = 0.012
spacing = 0.1
kinetic = 0.5 / (spacing * spacing)
block_scale = 90.0
dipole_scale = 40.0
laser_scale = 25.0

MESH = pl.DeviceIdType.MESH
F32, BF16 = jnp.float32, jnp.bfloat16
NT = (((1,), (1,)), ((), ()))

SYM, DEV = 4, 64
TOP = 8


def torus(step):
    return min(step, 4 - step)


OFFSETS = sorted(
    [(oy, ox) for oy in range(4) for ox in range(4) if (oy, ox) != (0, 0)],
    key=lambda o: -(torus(o[0]) + torus(o[1])),
)


def added(terms):
    chains = [terms[n].astype(F32) for n in range(8)]
    for n in range(8, len(terms)):
        chains[n % 8] += terms[n].astype(F32)
    while len(chains) > 1:
        chains = [chains[n] + chains[n + 1] for n in range(0, len(chains), 2)]
    return chains[0]


def remote(src, dst, send, recv, sym, dev):
    return pltpu.make_async_remote_copy(
        src_ref=src, dst_ref=dst, send_sem=send, recv_sem=recv, device_id=(sym, dev), device_id_type=MESH
    )


def drain(ref, sem):
    pltpu.make_async_copy(ref, ref, sem).wait()


def kernel(
    sizes_in, inner, ham, dip, amps, chan, outer, energy, laser,
    inner_out, outer_out,
    sizes, inn, mats, dips, ampv, chv, out_raw, env, lasv, u, acc, wsum,
    stage1, got1, stage2, own, stage3, above, stage4, below,
    staged, first2, got, above_d, below_d, lows, highs, lower_h, upper_h,
    bst, bgot, bst2, bgot2, sgot,
    load, halo_send, halo_recv, send1, recv1, send2, recv2, send3, recv3, send4, recv4,
    sendd, recvd, sendx, recvx, sendh, recvh,
    bsend, brecv, bsend2, brecv2, ssend, srecv, ssend2,
):
    s = lax.axis_index("sym")
    d = lax.axis_index("dev")
    y, zl, x = d // 16, (d // 4) % 4, d % 4
    plane = y * 4 + x
    parity = x % 2
    group = s * 4 + zl
    is_plane_root = plane == 0
    is_root = jnp.logical_and(s == 0, d == 0)
    is_last = jnp.logical_and(s == SYM - 1, d == DEV - 1)
    channels = ampv.shape[1]
    points = out_raw.shape[2]
    rows = u.shape[1]

    def dev_of(y_, z_, x_):
        return (y_ * 4 + z_) * 4 + x_

    pairs = (
        (sizes_in, sizes), (inner, inn), (dip, dips), (amps, ampv), (chan, chv),
        (outer, out_raw), (energy, env), (laser, lasv), (ham, mats),
    )
    loads = [pltpu.make_async_copy(src, dst, load.at[n]) for n, (src, dst) in enumerate(pairs)]
    for one in loads[:3]:
        one.start()

    barrier = pltpu.get_barrier_semaphore()

    def greet(sym, dev):
        pl.semaphore_signal(barrier, inc=1, device_id=(sym, dev), device_id_type=MESH)

    for oy, ox in OFFSETS:
        greet(s, dev_of((y + oy) % 4, zl, (x + ox) % 4))
    for oz in range(1, 4):
        greet(s, dev_of(y, (zl + oz) % 4, x))
    expected = jnp.int32(18)
    has_below = s > 0
    has_above = s < SYM - 1

    @pl.when(has_below)
    def _():
        for z_ in range(4):
            greet(s - 1, dev_of(y, z_, x))

    @pl.when(has_above)
    def _():
        for z_ in range(4):
            greet(s + 1, dev_of(y, z_, x))

    expected += 4 * has_below.astype(jnp.int32) + 4 * has_above.astype(jnp.int32)

    @pl.when(is_root)
    def _():
        for g in range(1, 16):
            greet(jnp.int32(g // 4), jnp.int32((g % 4) * 4))

    hears_root = jnp.logical_and(is_plane_root, jnp.logical_not(is_root))

    @pl.when(hears_root)
    def _():
        greet(jnp.int32(0), jnp.int32(0))

    expected += 15 * is_root.astype(jnp.int32) + hears_root.astype(jnp.int32)
    position = s * DEV + d
    left, right = position - 1, position + 1
    has_left = jnp.logical_not(is_root)
    has_right = jnp.logical_not(is_last)

    @pl.when(has_left)
    def _():
        greet(left // DEV, left % DEV)

    @pl.when(has_right)
    def _():
        greet(right // DEV, right % DEV)

    expected += has_left.astype(jnp.int32) + has_right.astype(jnp.int32)

    for one in loads[3:]:
        one.start()

    for one in loads[0:3]:
        one.wait()
    size0, size1 = sizes[2 * s], sizes[2 * s + 1]
    row_index = d * 64 + lax.broadcasted_iota(jnp.int32, (2, 64), 1)
    live0 = row_index < size0
    live1 = row_index < size1
    zero2 = jnp.zeros((2, 64), BF16)
    zero4 = jnp.zeros((4, 64), BF16)

    def products(state):
        half = state.astype(BF16)
        spread = jnp.concatenate(
            [jnp.concatenate([half[0:2], zero2], axis=1), jnp.concatenate([zero2, half[2:4]], axis=1)], axis=0
        )
        flat = dips[...].reshape(128, dips.shape[2])
        part = jnp.dot(spread, flat, preferred_element_type=F32).astype(BF16)
        even = jnp.concatenate([half, zero4], axis=1)
        odd = jnp.concatenate([zero4, half], axis=1)
        chunk = jnp.where(parity == 0, even, odd)
        return chunk, part

    def stage_boundary(state):
        per_block = jnp.dot(state.astype(BF16), ampv[...], preferred_element_type=F32)
        bst[...] = owned0 * per_block[0:2] + owned1 * per_block[2:4]

    def prepare_plane(state):
        chunk, part = products(state)
        for y_ in range(4):
            for xh in range(2):
                stage1[y_ * 2 + xh, 0] = chunk
                for z_ in range(4):
                    tile = (y_ * 4 + z_) * 2 + xh
                    stage1[y_ * 2 + xh, 1 + z_] = part[:, tile * 128 : (tile + 1) * 128]

    def prepare_direct(state):
        chunk, part = products(state)
        first2[...] = chunk[0:2]
        for tile in range(32):
            staged[tile, 0] = chunk
            staged[tile, 1] = part[:, tile * 128 : (tile + 1) * 128]

    first = jnp.concatenate(
        [jnp.where(live0, inn[0], 0.0), jnp.where(live1, inn[1], 0.0)], axis=0
    )
    wsum[...] = first
    loads[3].wait()
    loads[4].wait()
    owned0 = (chv[...] == 2 * s).astype(F32)
    owned1 = (chv[...] == 2 * s + 1).astype(F32)
    prepare_plane(first)
    stage_boundary(first)

    def slope_of(i):
        near = u[i, TOP : TOP + 8, :]
        return (-3.0 * near[0:1] + 4.0 * near[1:2] - near[2:3]) * (0.5 / spacing)

    def stage_slope(k):
        both = jnp.concatenate([slope_of(0), slope_of(1)], axis=0)
        sgot[k] = both.astype(BF16)

    line = lax.broadcasted_iota(jnp.int32, (rows, 1), 0)
    inside = jnp.logical_and(
        jnp.logical_or(line >= TOP, has_left), jnp.logical_or(line < TOP + points, has_right)
    )

    to_left = remote(
        u.at[:, pl.ds(TOP, 8), :], u.at[:, pl.ds(TOP + points, 8), :],
        halo_send.at[0], halo_recv.at[0], left // DEV, left % DEV,
    )
    to_right = remote(
        u.at[:, pl.ds(points, 8), :], u.at[:, pl.ds(0, 8), :],
        halo_send.at[1], halo_recv.at[1], right // DEV, right % DEV,
    )

    def slope_to(k, g):
        return remote(
            sgot.at[k], sgot.at[k], ssend.at[g], srecv.at[k], jnp.int32(g // 4), jnp.int32((g % 4) * 4)
        )

    def slope_on(k, n):
        oy, ox = OFFSETS[n]
        return remote(sgot.at[k], sgot.at[k], ssend2.at[n], srecv.at[k], s, dev_of(oy, zl, ox))

    def factor_of(k):
        return time_step / (k + 1) if isinstance(k, int) else time_step / (k + 1).astype(F32)

    def edge_of(k):
        drain(bgot2.at[k, pl.ds(0, 15)], brecv2.at[k])
        edge = jnp.sum(bgot2[k], axis=0) * (-kinetic * factor_of(k))
        return edge[1:2], -edge[0:1]

    def send_boundary(k):
        @pl.when(is_plane_root)
        def _():
            bgot[k, 0] = bst[...]

        @pl.when(jnp.logical_not(is_plane_root))
        def _():
            remote(bst, bgot.at[k, plane], bsend, brecv.at[k], s, dev_of(0, zl, 0)).start()

    def send_slope(k):
        for g in range(1, 16):
            slope_to(k, g).start()

    def relay(k):
        @pl.when(hears_root)
        def _():
            drain(sgot.at[k], srecv.at[k])

        for n in range(15):
            slope_on(k, n).start()
        drain(bgot.at[k, pl.ds(0, 15)], brecv.at[k])
        total = jnp.sum(bgot[k], axis=0)

        @pl.when(is_root)
        def _():
            bgot2[k, 0] = total

        @pl.when(hears_root)
        def _():
            bst2[...] = total
            remote(bst2, bgot2.at[k, group], bsend2, brecv2.at[k], jnp.int32(0), jnp.int32(0)).start()

    def outer_update(k):
        factor = factor_of(k)
        images = []
        levels = env[...].reshape(1, channels)
        for i in range(2):
            value = u[i]
            mixed = jnp.dot(value.astype(BF16), lasv[...], preferred_element_type=F32)
            curve = pltpu.roll(value, 1, 0) - 2.0 * value + pltpu.roll(value, rows - 1, 0)
            image = -kinetic * curve + levels * value + laser_scale * mixed
            images.append(jnp.where(inside, image, 0.0))
        new0 = factor * images[1]
        new1 = -factor * images[0]
        u[0] = new0
        u[1] = new1
        acc[0] += new0[TOP : TOP + points]
        acc[1] += new1[TOP : TOP + points]

    def times(vectors, matrix):
        return lax.dot_general(vectors, matrix, NT, preferred_element_type=F32)

    def half_of(tile):
        return jnp.where(parity == 0, tile[:, 0:64], tile[:, 64:128])

    def slope_term(k):
        @pl.when(jnp.logical_not(is_plane_root))
        def _():
            drain(sgot.at[k], srecv.at[k])

        slope = sgot[k].astype(F32)
        masked = jnp.concatenate([owned0 * slope, owned1 * slope], axis=0).astype(BF16)
        return lax.dot_general(masked, ampv[...], NT, preferred_element_type=F32)

    def next_slope(k):
        fixes = edge_of(k)
        slopes = [slope_of(i) - (1.5 / spacing) * fixes[i] for i in range(2)]
        sgot[k + 1] = jnp.concatenate(slopes, axis=0).astype(BF16)
        send_slope(k + 1)
        for i in range(2):
            u[i, TOP : TOP + 1, :] += fixes[i]
            acc[i, 0:1, :] += fixes[i]

    def last_column(k):
        fixes = edge_of(k)
        columns = jnp.transpose(jnp.concatenate([*fixes, jnp.zeros((6, channels), F32)], axis=0))
        for i in range(2):
            outer_out[i, :, 0:1] += columns[:, i : i + 1]

    def finish(k, image0, image1):
        image0 = jnp.where(live0, image0, 0.0)
        image1 = jnp.where(live1, image1, 0.0)
        fresh = factor_of(k) * jnp.concatenate(
            [image0[1:2], -image0[0:1], image1[1:2], -image1[0:1]], axis=0
        )
        wsum[...] += fresh

        @pl.when(jnp.logical_not(is_plane_root))
        def _():
            drain(bst, bsend)

        def ahead():
            stage_boundary(fresh)
            send_boundary(k + 1)

        if isinstance(k, int):
            ahead()
        else:
            pl.when(k < TERMS - 1)(ahead)
        return fresh

    def sent_slope(k):
        @pl.when(is_plane_root)
        def _():
            for n in range(15):
                slope_on(k, n).wait_send()

        @pl.when(is_root)
        def _():
            for g in range(1, 16):
                slope_to(k, g).wait_send()

        @pl.when(hears_root)
        def _():
            drain(bst2, bsend2)

    pl.semaphore_wait(barrier, expected)

    send_boundary(0)
    for n, (oy, ox) in enumerate(OFFSETS):
        ty, tx = (y + oy) % 4, (x + ox) % 4
        remote(
            stage1.at[ty * 2 + tx // 2], got1.at[plane], send1, recv1, s, dev_of(ty, zl, tx)
        ).start()

    loads[5].wait()
    blank = jnp.zeros((2, TOP, channels), F32)

    @pl.when(is_root)
    def _():
        u[:, 0:TOP, :] = blank

    @pl.when(is_last)
    def _():
        u[:, TOP + points : rows, :] = blank

    for i in range(2):
        turned = jnp.transpose(out_raw[i])
        u[i, TOP : TOP + points, :] = turned
        acc[i] = turned

    @pl.when(is_root)
    def _():
        stage_slope(0)
        send_slope(0)

    @pl.when(has_left)
    def _():
        to_left.start()

    @pl.when(has_right)
    def _():
        to_right.start()

    for one in loads[6:9]:
        one.wait()
    got1[plane] = stage1[y * 2 + x // 2]
    drain(got1.at[pl.ds(0, 15)], recv1)

    sums = added([got1[p, 1:5] for p in range(16)]).astype(BF16)
    tiles = [got1[2 * q, 0] + got1[2 * q + 1, 0] for q in range(8)]
    for z_ in range(4):
        for q in range(8):
            stage2[z_, q] = tiles[q]
        stage2[z_, 8] = sums[z_]
        stage4[z_] = sums[z_]
    for q in range(8):
        stage3[q] = tiles[q][0:2]

    @pl.when(has_below)
    def _():
        for z_ in range(4):
            remote(stage3, above.at[zl], send3, recv3, s - 1, dev_of(y, z_, x)).start()

    @pl.when(has_above)
    def _():
        for z_ in range(4):
            remote(stage4.at[z_], below.at[zl], send4, recv4, s + 1, dev_of(y, z_, x)).start()

    for oz in (2, 1, 3):
        tz = (zl + oz) % 4
        remote(stage2.at[tz], own.at[zl], send2, recv2, s, dev_of(y, tz, x)).start()
    own[zl] = stage2[zl]

    @pl.when(is_plane_root)
    def _():
        relay(0)

    @pl.when(has_left)
    def _():
        to_right.wait_recv()
        to_left.wait_send()

    @pl.when(has_right)
    def _():
        to_left.wait_recv()
        to_right.wait_send()

    outer_update(0)

    drain(own.at[pl.ds(0, 3)], recv2)

    @pl.when(has_above)
    def _():
        drain(above, recv3)

    @pl.when(has_below)
    def _():
        drain(below, recv4)

    order = [(y_, z_, xh) for y_ in range(4) for z_ in range(4) for xh in range(2)]
    mine = jnp.concatenate([own[z_, y_ * 2 + xh] for y_, z_, xh in order], axis=1)
    upper = jnp.concatenate([above[z_, y_ * 2 + xh] for y_, z_, xh in order], axis=1)
    lower0 = below[0].astype(F32)
    lower1 = own[0, 8].astype(F32)
    for z_ in range(1, 4):
        lower0 += below[z_].astype(F32)
        lower1 += own[z_, 8].astype(F32)
    lower0 = jnp.where(has_below, half_of(lower0)[2:4], 0.0)
    lower1 = half_of(lower1)[0:2]
    forward1 = jnp.where(has_above, times(upper, dips[1]), 0.0)
    image0 = block_scale * times(mine, mats[0])[0:2] + dipole_scale * (times(mine, dips[0])[2:4] + lower0)
    image1 = block_scale * times(mine, mats[1])[2:4] + dipole_scale * (forward1 + lower1)
    bloch = slope_term(0)
    fresh = finish(0, image0 + bloch[0:2], image1 + bloch[2:4])

    @pl.when(is_root)
    def _():
        next_slope(0)

    prepare_direct(fresh)
    drain(got1.at[pl.ds(0, 15)], send1)
    drain(own.at[pl.ds(0, 3)], send2)

    @pl.when(has_below)
    def _():
        drain(above, send3)

    @pl.when(has_above)
    def _():
        drain(below, send4)

    sent_slope(0)
    partner = s + 1 - 2 * (s % 2)
    is_low = s % 2 == 0
    is_high = s % 2 == 1

    @pl.loop(1, TERMS)
    def _(k):
        for level in range(4, -1, -1):
            ring = [o for o in OFFSETS + [(0, 0)] if torus(o[0]) + torus(o[1]) == level]
            targets = [
                (dev_of((y + oy) % 4, (zl + oz) % 4, (x + ox) % 4), (oy, oz, ox)) for oz in (2, 1, 3, 0) for oy, ox in ring
            ]

            @pl.when(s == 1)
            def _():
                for to, _o in targets:
                    remote(staged.at[to // 2, 1], below_d.at[k, d], sendx, recvx.at[k], jnp.int32(2), to).start()

            @pl.when(s == 2)
            def _():
                for to, _o in targets:
                    remote(first2, above_d.at[k, d], sendx, recvx.at[k], jnp.int32(1), to).start()

            for to, offset in targets:
                if offset != (0, 0, 0):
                    remote(staged.at[to // 2], got.at[k, d], sendd, recvd.at[k], s, to).start()

        got[k, d] = staged[d // 2]

        @pl.when(is_plane_root)
        def _():
            relay(k)

        outer_update(k)

        @pl.when(k == TERMS - 1)
        def _():
            for i in range(2):
                outer_out[i] = jnp.transpose(acc[i])

        drain(got.at[k, pl.ds(0, 63)], recvd.at[k])
        give_low = remote(lows, lower_h.at[k], sendh, recvh.at[k], partner, d)
        give_high = remote(highs, upper_h.at[k], sendh, recvh.at[k], partner, d)

        @pl.when(is_high)
        def _():
            for q in range(32):
                highs[:, q * 128 : (q + 1) * 128] = got[k, 2 * q, 0, 0:2] + got[k, 2 * q + 1, 0, 0:2]
            give_high.start()

        sums = added([got[k, p, 1] for p in range(64)])

        @pl.when(is_low)
        def _():
            lows[...] = sums[2:4]
            give_low.start()

        mine = jnp.concatenate([got[k, 2 * q, 0] + got[k, 2 * q + 1, 0] for q in range(32)], axis=1)
        image0 = block_scale * times(mine, mats[0])[0:2] + dipole_scale * times(mine, dips[0])[2:4]
        image1 = block_scale * times(mine, mats[1])[2:4] + dipole_scale * half_of(sums)[0:2]
        bloch = slope_term(k)
        image0 += bloch[0:2]
        image1 += bloch[2:4]

        @pl.when(jnp.logical_and(is_root, k < TERMS - 1))
        def _():
            next_slope(k)

        @pl.when(jnp.logical_and(is_root, k == TERMS - 1))
        def _():
            last_column(k)

        @pl.when(s == 1)
        def _():
            drain(above_d.at[k], recvx.at[k])
            for q in range(32):
                upper_h[k, :, q * 128 : (q + 1) * 128] = above_d[k, 2 * q] + above_d[k, 2 * q + 1]

        @pl.when(s == 2)
        def _():
            drain(below_d.at[k], recvx.at[k])
            lower_h[k] = added([below_d[k, p] for p in range(64)])[2:4]

        @pl.when(is_low)
        def _():
            drain(upper_h.at[k], recvh.at[k])

        @pl.when(is_high)
        def _():
            drain(lower_h.at[k], recvh.at[k])

        image0 += jnp.where(has_below, dipole_scale * half_of(lower_h[k]), 0.0)
        image1 += jnp.where(has_above, dipole_scale * times(upper_h[k], dips[1]), 0.0)
        fresh = finish(k, image0, image1)

        drain(got.at[k, pl.ds(0, 63)], sendd)

        @pl.when(s == 1)
        def _():
            drain(below_d.at[k], sendx)

        @pl.when(s == 2)
        def _():
            drain(above_d.at[k], sendx)

        @pl.when(k < TERMS - 1)
        def _():
            prepare_direct(fresh)

        @pl.when(is_low)
        def _():
            drain(lower_h.at[k], sendh)

        @pl.when(is_high)
        def _():
            drain(upper_h.at[k], sendh)

        sent_slope(k)

    inner_out[0] = wsum[0:2]
    inner_out[1] = wsum[2:4]


def deliver(inner_v, outer_v, inner_out, outer_out, sems):
    copies = [
        pltpu.make_async_copy(outer_v, outer_out, sems.at[0]),
        pltpu.make_async_copy(inner_v, inner_out, sems.at[1]),
    ]
    for one in copies:
        one.start()
    for one in copies:
        one.wait()


def on_device(inner, sizes, ham, dip, amps, chan, outer, energy, laser):
    blocks, parts, own_rows = inner.shape
    states = ham.shape[2]
    channels, points = outer.shape[1], outer.shape[2]
    rows = points + 16
    dma = pltpu.SemaphoreType.DMA
    anywhere = pl.BlockSpec(memory_space=pl.ANY)
    results = pl.pallas_call(
        kernel,
        out_shape=(
            pltpu.VMEM(inner.shape, F32),
            pltpu.VMEM(outer.shape, F32),
        ),
        in_specs=[anywhere] * 9,
        out_specs=(pl.BlockSpec(memory_space=pltpu.VMEM), pl.BlockSpec(memory_space=pltpu.VMEM)),
        scratch_shapes=[
            pltpu.SMEM(sizes.shape, jnp.int32),
            pltpu.VMEM(inner.shape, F32),
            pltpu.VMEM(ham.shape, BF16),
            pltpu.VMEM(dip.shape, BF16),
            pltpu.VMEM((own_rows, channels), BF16),
            pltpu.VMEM((1, channels), jnp.int32),
            pltpu.VMEM(outer.shape, F32),
            pltpu.VMEM((channels,), F32),
            pltpu.VMEM(laser.shape, BF16),
            pltpu.VMEM((2, rows, channels), F32),
            pltpu.VMEM((2, points, channels), F32),
            pltpu.VMEM((4, own_rows), F32),
            pltpu.VMEM((8, 5, 4, 128), BF16),
            pltpu.VMEM((16, 5, 4, 128), BF16),
            pltpu.VMEM((4, 9, 4, 128), BF16),
            pltpu.VMEM((4, 9, 4, 128), BF16),
            pltpu.VMEM((8, 2, 128), BF16),
            pltpu.VMEM((4, 8, 2, 128), BF16),
            pltpu.VMEM((4, 4, 128), BF16),
            pltpu.VMEM((4, 4, 128), BF16),
            pltpu.VMEM((32, 2, 4, 128), BF16),
            pltpu.VMEM((2, 128), BF16),
            pltpu.VMEM((TERMS, 64, 2, 4, 128), BF16),
            pltpu.VMEM((TERMS, 64, 2, 128), BF16),
            pltpu.VMEM((TERMS, 64, 4, 128), BF16),
            pltpu.VMEM((2, 128), F32),
            pltpu.VMEM((2, states), BF16),
            pltpu.VMEM((TERMS, 2, 128), F32),
            pltpu.VMEM((TERMS, 2, states), BF16),
            pltpu.VMEM((2, channels), F32),
            pltpu.VMEM((TERMS, 16, 2, channels), F32),
            pltpu.VMEM((2, channels), F32),
            pltpu.VMEM((TERMS, 16, 2, channels), F32),
            pltpu.VMEM((TERMS, 2, channels), BF16),
            dma((9,)), dma((2,)), dma((2,)),
            dma, dma, dma, dma, dma, dma, dma, dma,
            dma, dma((TERMS,)), dma, dma((TERMS,)), dma, dma((TERMS,)),
            dma, dma((TERMS,)), dma, dma((TERMS,)), dma((16,)), dma((TERMS,)), dma((15,)),
        ],
        compiler_params=pltpu.CompilerParams(
            collective_id=0, has_side_effects=True, vmem_limit_bytes=60 * 1024 * 1024
        ),
    )(
        sizes, inner, ham, dip, amps.T, chan.reshape(1, channels), outer, energy, laser,
    )
    return pl.pallas_call(
        deliver,
        out_shape=(
            jax.ShapeDtypeStruct(inner.shape, F32),
            jax.ShapeDtypeStruct(outer.shape, F32),
        ),
        in_specs=[pl.BlockSpec(memory_space=pltpu.VMEM)] * 2,
        out_specs=(anywhere, anywhere),
        scratch_shapes=[dma((2,))],
        compiler_params=pltpu.CompilerParams(vmem_limit_bytes=1024 * 1024),
    )(*results)


def solution(mesh):
    placed = (
        P("sym", None, "dev"),
        P(),
        P("sym", "dev", None),
        P("sym", "dev", None),
        P(None, "dev"),
        P(),
        P(None, None, ("sym", "dev")),
        P(),
        P(),
    )
    return jax.shard_map(
        on_device,
        mesh=mesh,
        in_specs=placed,
        out_specs=(P("sym", None, "dev"), P(None, None, ("sym", "dev"))),
        check_vma=False,
    )
```

```python
import functools

import jax
import jax.numpy as jnp
from jax import lax
from jax.experimental import pallas as pl
from jax.experimental.pallas import tpu as pltpu
from jax.sharding import PartitionSpec as P

TERMS = 4
time_step = 0.012
spacing = 0.1
kinetic = 0.5 / (spacing * spacing)
block_scale = 90.0
dipole_scale = 40.0
laser_scale = 25.0

MESH = pl.DeviceIdType.MESH
F32, BF16 = jnp.float32, jnp.bfloat16
NT = (((1,), (1,)), ((), ()))

SYM, DEV = 4, 64
TOP = 8


def torus(step):
    return min(step, 4 - step)


OFFSETS = sorted(
    [(oy, ox) for oy in range(4) for ox in range(4) if (oy, ox) != (0, 0)],
    key=lambda o: -(torus(o[0]) + torus(o[1])),
)


def added(terms):
    chains = [terms[n].astype(F32) for n in range(8)]
    for n in range(8, len(terms)):
        chains[n % 8] += terms[n].astype(F32)
    while len(chains) > 1:
        chains = [chains[n] + chains[n + 1] for n in range(0, len(chains), 2)]
    return chains[0]


def remote(src, dst, send, recv, sym, dev):
    return pltpu.make_async_remote_copy(
        src_ref=src, dst_ref=dst, send_sem=send, recv_sem=recv, device_id=(sym, dev), device_id_type=MESH
    )


def drain(ref, sem):
    pltpu.make_async_copy(ref, ref, sem).wait()


def kernel(
    sizes_in, inner, ham, dip, amps, chan, outer, energy, laser,
    inner_out, outer_out,
    sizes, inn, mats, dips, ampv, chv, out_raw, env, lasv, u, acc, wsum,
    stage1, got1, stage2, own, stage3, above, stage4, below,
    staged, first2, got, above_d, below_d, lows, highs, lower_h, upper_h,
    bst, bgot, bst2, bgot2, sgot,
    load, halo_send, halo_recv, send1, recv1, send2, recv2, send3, recv3, send4, recv4,
    sendd, recvd, sendx, recvx, sendh, recvh,
    bsend, brecv, bsend2, brecv2, ssend, srecv, ssend2,
):
    s = lax.axis_index("sym")
    d = lax.axis_index("dev")
    y, zl, x = d // 16, (d // 4) % 4, d % 4
    plane = y * 4 + x
    parity = x % 2
    group = s * 4 + zl
    is_plane_root = plane == 0
    is_root = jnp.logical_and(s == 0, d == 0)
    is_last = jnp.logical_and(s == SYM - 1, d == DEV - 1)
    channels = ampv.shape[1]
    points = out_raw.shape[2]
    rows = u.shape[1]

    def dev_of(y_, z_, x_):
        return (y_ * 4 + z_) * 4 + x_

    pairs = (
        (sizes_in, sizes), (inner, inn), (dip, dips), (amps, ampv), (chan, chv),
        (outer, out_raw), (energy, env), (laser, lasv), (ham, mats),
    )
    loads = [pltpu.make_async_copy(src, dst, load.at[n]) for n, (src, dst) in enumerate(pairs)]
    for one in loads[:3]:
        one.start()

    barrier = pltpu.get_barrier_semaphore()

    def greet(sym, dev):
        pl.semaphore_signal(barrier, inc=1, device_id=(sym, dev), device_id_type=MESH)

    for oy, ox in OFFSETS:
        greet(s, dev_of((y + oy) % 4, zl, (x + ox) % 4))
    for oz in range(1, 4):
        greet(s, dev_of(y, (zl + oz) % 4, x))
    expected = jnp.int32(18)
    has_below = s > 0
    has_above = s < SYM - 1

    @pl.when(has_below)
    def _():
        for z_ in range(4):
            greet(s - 1, dev_of(y, z_, x))

    @pl.when(has_above)
    def _():
        for z_ in range(4):
            greet(s + 1, dev_of(y, z_, x))

    expected += 4 * has_below.astype(jnp.int32) + 4 * has_above.astype(jnp.int32)

    @pl.when(is_root)
    def _():
        for g in range(1, 16):
            greet(jnp.int32(g // 4), jnp.int32((g % 4) * 4))

    hears_root = jnp.logical_and(is_plane_root, jnp.logical_not(is_root))

    @pl.when(hears_root)
    def _():
        greet(jnp.int32(0), jnp.int32(0))

    expected += 15 * is_root.astype(jnp.int32) + hears_root.astype(jnp.int32)
    position = s * DEV + d
    left, right = position - 1, position + 1
    has_left = jnp.logical_not(is_root)
    has_right = jnp.logical_not(is_last)

    @pl.when(has_left)
    def _():
        greet(left // DEV, left % DEV)

    @pl.when(has_right)
    def _():
        greet(right // DEV, right % DEV)

    expected += has_left.astype(jnp.int32) + has_right.astype(jnp.int32)

    for one in loads[3:]:
        one.start()

    for one in loads[0:3]:
        one.wait()
    size0, size1 = sizes[2 * s], sizes[2 * s + 1]
    row_index = d * 64 + lax.broadcasted_iota(jnp.int32, (2, 64), 1)
    live0 = row_index < size0
    live1 = row_index < size1
    zero2 = jnp.zeros((2, 64), BF16)
    zero4 = jnp.zeros((4, 64), BF16)

    def products(state):
        half = state.astype(BF16)
        spread = jnp.concatenate(
            [jnp.concatenate([half[0:2], zero2], axis=1), jnp.concatenate([zero2, half[2:4]], axis=1)], axis=0
        )
        flat = dips[...].reshape(128, dips.shape[2])
        part = jnp.dot(spread, flat, preferred_element_type=F32).astype(BF16)
        even = jnp.concatenate([half, zero4], axis=1)
        odd = jnp.concatenate([zero4, half], axis=1)
        chunk = jnp.where(parity == 0, even, odd)
        return chunk, part

    def stage_boundary(state):
        per_block = jnp.dot(state.astype(BF16), ampv[...], preferred_element_type=F32)
        bst[...] = owned0 * per_block[0:2] + owned1 * per_block[2:4]

    def prepare_plane(state):
        chunk, part = products(state)
        for y_ in range(4):
            for xh in range(2):
                stage1[y_ * 2 + xh, 0] = chunk
                for z_ in range(4):
                    tile = (y_ * 4 + z_) * 2 + xh
                    stage1[y_ * 2 + xh, 1 + z_] = part[:, tile * 128 : (tile + 1) * 128]

    def prepare_direct(state):
        chunk, part = products(state)
        first2[...] = chunk[0:2]
        for tile in range(32):
            staged[tile, 0] = chunk
            staged[tile, 1] = part[:, tile * 128 : (tile + 1) * 128]

    first = jnp.concatenate(
        [jnp.where(live0, inn[0], 0.0), jnp.where(live1, inn[1], 0.0)], axis=0
    )
    wsum[...] = first
    loads[3].wait()
    loads[4].wait()
    owned0 = (chv[...] == 2 * s).astype(F32)
    owned1 = (chv[...] == 2 * s + 1).astype(F32)
    prepare_plane(first)
    stage_boundary(first)

    def slope_of(i):
        near = u[i, TOP : TOP + 8, :]
        return (-3.0 * near[0:1] + 4.0 * near[1:2] - near[2:3]) * (0.5 / spacing)

    def stage_slope(k):
        both = jnp.concatenate([slope_of(0), slope_of(1)], axis=0)
        sgot[k] = both.astype(BF16)

    line = lax.broadcasted_iota(jnp.int32, (rows, 1), 0)
    inside = jnp.logical_and(
        jnp.logical_or(line >= TOP, has_left), jnp.logical_or(line < TOP + points, has_right)
    )

    to_left = remote(
        u.at[:, pl.ds(TOP, 8), :], u.at[:, pl.ds(TOP + points, 8), :],
        halo_send.at[0], halo_recv.at[0], left // DEV, left % DEV,
    )
    to_right = remote(
        u.at[:, pl.ds(points, 8), :], u.at[:, pl.ds(0, 8), :],
        halo_send.at[1], halo_recv.at[1], right // DEV, right % DEV,
    )

    def slope_to(k, g):
        return remote(
            sgot.at[k], sgot.at[k], ssend.at[g], srecv.at[k], jnp.int32(g // 4), jnp.int32((g % 4) * 4)
        )

    def slope_on(k, n):
        oy, ox = OFFSETS[n]
        return remote(sgot.at[k], sgot.at[k], ssend2.at[n], srecv.at[k], s, dev_of(oy, zl, ox))

    def factor_of(k):
        return time_step / (k + 1) if isinstance(k, int) else time_step / (k + 1).astype(F32)

    def edge_of(k):
        drain(bgot2.at[k, pl.ds(0, 15)], brecv2.at[k])
        edge = jnp.sum(bgot2[k], axis=0) * (-kinetic * factor_of(k))
        return edge[1:2], -edge[0:1]

    def send_boundary(k):
        @pl.when(is_plane_root)
        def _():
            bgot[k, 0] = bst[...]

        @pl.when(jnp.logical_not(is_plane_root))
        def _():
            remote(bst, bgot.at[k, plane], bsend, brecv.at[k], s, dev_of(0, zl, 0)).start()

    def send_slope(k):
        for g in range(1, 16):
            slope_to(k, g).start()

    def relay(k):
        @pl.when(hears_root)
        def _():
            drain(sgot.at[k], srecv.at[k])

        for n in range(15):
            slope_on(k, n).start()
        drain(bgot.at[k, pl.ds(0, 15)], brecv.at[k])
        total = jnp.sum(bgot[k], axis=0)

        @pl.when(is_root)
        def _():
            bgot2[k, 0] = total

        @pl.when(hears_root)
        def _():
            bst2[...] = total
            remote(bst2, bgot2.at[k, group], bsend2, brecv2.at[k], jnp.int32(0), jnp.int32(0)).start()

    def outer_update(k):
        factor = factor_of(k)
        images = []
        levels = env[...].reshape(1, channels)
        for i in range(2):
            value = u[i]
            mixed = jnp.dot(value.astype(BF16), lasv[...], preferred_element_type=F32)
            curve = pltpu.roll(value, 1, 0) - 2.0 * value + pltpu.roll(value, rows - 1, 0)
            image = -kinetic * curve + levels * value + laser_scale * mixed
            images.append(jnp.where(inside, image, 0.0))
        new0 = factor * images[1]
        new1 = -factor * images[0]
        u[0] = new0
        u[1] = new1
        acc[0] += new0[TOP : TOP + points]
        acc[1] += new1[TOP : TOP + points]

    def times(vectors, matrix):
        return lax.dot_general(vectors, matrix, NT, preferred_element_type=F32)

    def half_of(tile):
        return jnp.where(parity == 0, tile[:, 0:64], tile[:, 64:128])

    def slope_term(k):
        @pl.when(jnp.logical_not(is_plane_root))
        def _():
            drain(sgot.at[k], srecv.at[k])

        slope = sgot[k].astype(F32)
        masked = jnp.concatenate([owned0 * slope, owned1 * slope], axis=0).astype(BF16)
        return lax.dot_general(masked, ampv[...], NT, preferred_element_type=F32)

    def next_slope(k):
        fixes = edge_of(k)
        slopes = [slope_of(i) - (1.5 / spacing) * fixes[i] for i in range(2)]
        sgot[k + 1] = jnp.concatenate(slopes, axis=0).astype(BF16)
        send_slope(k + 1)
        for i in range(2):
            u[i, TOP : TOP + 1, :] += fixes[i]
            acc[i, 0:1, :] += fixes[i]

    def last_column(k):
        fixes = edge_of(k)
        columns = jnp.transpose(jnp.concatenate([*fixes, jnp.zeros((6, channels), F32)], axis=0))
        for i in range(2):
            outer_out[i, :, 0:1] += columns[:, i : i + 1]

    def finish(k, image0, image1):
        image0 = jnp.where(live0, image0, 0.0)
        image1 = jnp.where(live1, image1, 0.0)
        fresh = factor_of(k) * jnp.concatenate(
            [image0[1:2], -image0[0:1], image1[1:2], -image1[0:1]], axis=0
        )
        wsum[...] += fresh

        @pl.when(jnp.logical_not(is_plane_root))
        def _():
            drain(bst, bsend)

        def ahead():
            stage_boundary(fresh)
            send_boundary(k + 1)

        if isinstance(k, int):
            ahead()
        else:
            pl.when(k < TERMS - 1)(ahead)
        return fresh

    def sent_slope(k):
        @pl.when(is_plane_root)
        def _():
            for n in range(15):
                slope_on(k, n).wait_send()

        @pl.when(is_root)
        def _():
            for g in range(1, 16):
                slope_to(k, g).wait_send()

        @pl.when(hears_root)
        def _():
            drain(bst2, bsend2)

    pl.semaphore_wait(barrier, expected)

    send_boundary(0)
    for n, (oy, ox) in enumerate(OFFSETS):
        ty, tx = (y + oy) % 4, (x + ox) % 4
        remote(
            stage1.at[ty * 2 + tx // 2], got1.at[plane], send1, recv1, s, dev_of(ty, zl, tx)
        ).start()

    loads[5].wait()
    blank = jnp.zeros((2, TOP, channels), F32)

    @pl.when(is_root)
    def _():
        u[:, 0:TOP, :] = blank

    @pl.when(is_last)
    def _():
        u[:, TOP + points : rows, :] = blank

    for i in range(2):
        turned = jnp.transpose(out_raw[i])
        u[i, TOP : TOP + points, :] = turned
        acc[i] = turned

    @pl.when(is_root)
    def _():
        stage_slope(0)
        send_slope(0)

    @pl.when(has_left)
    def _():
        to_left.start()

    @pl.when(has_right)
    def _():
        to_right.start()

    for one in loads[6:9]:
        one.wait()
    got1[plane] = stage1[y * 2 + x // 2]
    drain(got1.at[pl.ds(0, 15)], recv1)

    sums = added([got1[p, 1:5] for p in range(16)]).astype(BF16)
    tiles = [got1[2 * q, 0] + got1[2 * q + 1, 0] for q in range(8)]
    for z_ in range(4):
        for q in range(8):
            stage2[z_, q] = tiles[q]
        stage2[z_, 8] = sums[z_]
        stage4[z_] = sums[z_]
    for q in range(8):
        stage3[q] = tiles[q][0:2]

    @pl.when(has_below)
    def _():
        for z_ in range(4):
            remote(stage3, above.at[zl], send3, recv3, s - 1, dev_of(y, z_, x)).start()

    @pl.when(has_above)
    def _():
        for z_ in range(4):
            remote(stage4.at[z_], below.at[zl], send4, recv4, s + 1, dev_of(y, z_, x)).start()

    for oz in (2, 1, 3):
        tz = (zl + oz) % 4
        remote(stage2.at[tz], own.at[zl], send2, recv2, s, dev_of(y, tz, x)).start()
    own[zl] = stage2[zl]

    @pl.when(is_plane_root)
    def _():
        relay(0)

    @pl.when(has_left)
    def _():
        to_right.wait_recv()
        to_left.wait_send()

    @pl.when(has_right)
    def _():
        to_left.wait_recv()
        to_right.wait_send()

    outer_update(0)

    drain(own.at[pl.ds(0, 3)], recv2)

    @pl.when(has_above)
    def _():
        drain(above, recv3)

    @pl.when(has_below)
    def _():
        drain(below, recv4)

    order = [(y_, z_, xh) for y_ in range(4) for z_ in range(4) for xh in range(2)]
    mine = jnp.concatenate([own[z_, y_ * 2 + xh] for y_, z_, xh in order], axis=1)
    upper = jnp.concatenate([above[z_, y_ * 2 + xh] for y_, z_, xh in order], axis=1)
    lower0 = below[0].astype(F32)
    lower1 = own[0, 8].astype(F32)
    for z_ in range(1, 4):
        lower0 += below[z_].astype(F32)
        lower1 += own[z_, 8].astype(F32)
    lower0 = jnp.where(has_below, half_of(lower0)[2:4], 0.0)
    lower1 = half_of(lower1)[0:2]
    forward1 = jnp.where(has_above, times(upper, dips[1]), 0.0)
    image0 = block_scale * times(mine, mats[0])[0:2] + dipole_scale * (times(mine, dips[0])[2:4] + lower0)
    image1 = block_scale * times(mine, mats[1])[2:4] + dipole_scale * (forward1 + lower1)
    bloch = slope_term(0)
    fresh = finish(0, image0 + bloch[0:2], image1 + bloch[2:4])

    @pl.when(is_root)
    def _():
        next_slope(0)

    prepare_direct(fresh)
    drain(got1.at[pl.ds(0, 15)], send1)
    drain(own.at[pl.ds(0, 3)], send2)

    @pl.when(has_below)
    def _():
        drain(above, send3)

    @pl.when(has_above)
    def _():
        drain(below, send4)

    sent_slope(0)
    partner = s + 1 - 2 * (s % 2)
    is_low = s % 2 == 0
    is_high = s % 2 == 1

    @pl.loop(1, TERMS)
    def _(k):
        for level in range(4, -1, -1):
            ring = [o for o in OFFSETS + [(0, 0)] if torus(o[0]) + torus(o[1]) == level]
            targets = [
                (dev_of((y + oy) % 4, (zl + oz) % 4, (x + ox) % 4), (oy, oz, ox)) for oz in (2, 1, 3, 0) for oy, ox in ring
            ]

            @pl.when(s == 1)
            def _():
                for to, _o in targets:
                    remote(staged.at[to // 2, 1], below_d.at[k, d], sendx, recvx.at[k], jnp.int32(2), to).start()

            @pl.when(s == 2)
            def _():
                for to, _o in targets:
                    remote(first2, above_d.at[k, d], sendx, recvx.at[k], jnp.int32(1), to).start()

            for to, offset in targets:
                if offset != (0, 0, 0):
                    remote(staged.at[to // 2], got.at[k, d], sendd, recvd.at[k], s, to).start()

        got[k, d] = staged[d // 2]

        @pl.when(is_plane_root)
        def _():
            relay(k)

        outer_update(k)

        @pl.when(k == TERMS - 1)
        def _():
            for i in range(2):
                outer_out[i] = jnp.transpose(acc[i])

        drain(got.at[k, pl.ds(0, 63)], recvd.at[k])
        give_low = remote(lows, lower_h.at[k], sendh, recvh.at[k], partner, d)
        give_high = remote(highs, upper_h.at[k], sendh, recvh.at[k], partner, d)

        @pl.when(is_high)
        def _():
            for q in range(32):
                highs[:, q * 128 : (q + 1) * 128] = got[k, 2 * q, 0, 0:2] + got[k, 2 * q + 1, 0, 0:2]
            give_high.start()

        sums = added([got[k, p, 1] for p in range(64)])

        @pl.when(is_low)
        def _():
            lows[...] = sums[2:4]
            give_low.start()

        mine = jnp.concatenate([got[k, 2 * q, 0] + got[k, 2 * q + 1, 0] for q in range(32)], axis=1)
        image0 = block_scale * times(mine, mats[0])[0:2] + dipole_scale * times(mine, dips[0])[2:4]
        image1 = block_scale * times(mine, mats[1])[2:4] + dipole_scale * half_of(sums)[0:2]
        bloch = slope_term(k)
        image0 += bloch[0:2]
        image1 += bloch[2:4]

        @pl.when(jnp.logical_and(is_root, k < TERMS - 1))
        def _():
            next_slope(k)

        @pl.when(jnp.logical_and(is_root, k == TERMS - 1))
        def _():
            last_column(k)

        @pl.when(s == 1)
        def _():
            drain(above_d.at[k], recvx.at[k])
            for q in range(32):
                upper_h[k, :, q * 128 : (q + 1) * 128] = above_d[k, 2 * q] + above_d[k, 2 * q + 1]

        @pl.when(s == 2)
        def _():
            drain(below_d.at[k], recvx.at[k])
            lower_h[k] = added([below_d[k, p] for p in range(64)])[2:4]

        @pl.when(is_low)
        def _():
            drain(upper_h.at[k], recvh.at[k])

        @pl.when(is_high)
        def _():
            drain(lower_h.at[k], recvh.at[k])

        image0 += jnp.where(has_below, dipole_scale * half_of(lower_h[k]), 0.0)
        image1 += jnp.where(has_above, dipole_scale * times(upper_h[k], dips[1]), 0.0)
        fresh = finish(k, image0, image1)

        drain(got.at[k, pl.ds(0, 63)], sendd)

        @pl.when(s == 1)
        def _():
            drain(below_d.at[k], sendx)

        @pl.when(s == 2)
        def _():
            drain(above_d.at[k], sendx)

        @pl.when(k < TERMS - 1)
        def _():
            prepare_direct(fresh)

        @pl.when(is_low)
        def _():
            drain(lower_h.at[k], sendh)

        @pl.when(is_high)
        def _():
            drain(upper_h.at[k], sendh)

        sent_slope(k)

    inner_out[0] = wsum[0:2]
    inner_out[1] = wsum[2:4]


def deliver(inner_v, outer_v, inner_out, outer_out, sems):
    copies = [
        pltpu.make_async_copy(outer_v.at[0], outer_out.at[0], sems.at[0]),
        pltpu.make_async_copy(outer_v.at[1], outer_out.at[1], sems.at[1]),
        pltpu.make_async_copy(inner_v, inner_out, sems.at[2]),
    ]
    for one in copies:
        one.start()
    for one in copies:
        one.wait()


def on_device(inner, sizes, ham, dip, amps, chan, outer, energy, laser):
    blocks, parts, own_rows = inner.shape
    states = ham.shape[2]
    channels, points = outer.shape[1], outer.shape[2]
    rows = points + 16
    dma = pltpu.SemaphoreType.DMA
    anywhere = pl.BlockSpec(memory_space=pl.ANY)
    results = pl.pallas_call(
        kernel,
        out_shape=(
            pltpu.VMEM(inner.shape, F32),
            pltpu.VMEM(outer.shape, F32),
        ),
        in_specs=[anywhere] * 9,
        out_specs=(pl.BlockSpec(memory_space=pltpu.VMEM), pl.BlockSpec(memory_space=pltpu.VMEM)),
        scratch_shapes=[
            pltpu.SMEM(sizes.shape, jnp.int32),
            pltpu.VMEM(inner.shape, F32),
            pltpu.VMEM(ham.shape, BF16),
            pltpu.VMEM(dip.shape, BF16),
            pltpu.VMEM((own_rows, channels), BF16),
            pltpu.VMEM((1, channels), jnp.int32),
            pltpu.VMEM(outer.shape, F32),
            pltpu.VMEM((channels,), F32),
            pltpu.VMEM(laser.shape, BF16),
            pltpu.VMEM((2, rows, channels), F32),
            pltpu.VMEM((2, points, channels), F32),
            pltpu.VMEM((4, own_rows), F32),
            pltpu.VMEM((8, 5, 4, 128), BF16),
            pltpu.VMEM((16, 5, 4, 128), BF16),
            pltpu.VMEM((4, 9, 4, 128), BF16),
            pltpu.VMEM((4, 9, 4, 128), BF16),
            pltpu.VMEM((8, 2, 128), BF16),
            pltpu.VMEM((4, 8, 2, 128), BF16),
            pltpu.VMEM((4, 4, 128), BF16),
            pltpu.VMEM((4, 4, 128), BF16),
            pltpu.VMEM((32, 2, 4, 128), BF16),
            pltpu.VMEM((2, 128), BF16),
            pltpu.VMEM((TERMS, 64, 2, 4, 128), BF16),
            pltpu.VMEM((TERMS, 64, 2, 128), BF16),
            pltpu.VMEM((TERMS, 64, 4, 128), BF16),
            pltpu.VMEM((2, 128), F32),
            pltpu.VMEM((2, states), BF16),
            pltpu.VMEM((TERMS, 2, 128), F32),
            pltpu.VMEM((TERMS, 2, states), BF16),
            pltpu.VMEM((2, channels), F32),
            pltpu.VMEM((TERMS, 16, 2, channels), F32),
            pltpu.VMEM((2, channels), F32),
            pltpu.VMEM((TERMS, 16, 2, channels), F32),
            pltpu.VMEM((TERMS, 2, channels), BF16),
            dma((9,)), dma((2,)), dma((2,)),
            dma, dma, dma, dma, dma, dma, dma, dma,
            dma, dma((TERMS,)), dma, dma((TERMS,)), dma, dma((TERMS,)),
            dma, dma((TERMS,)), dma, dma((TERMS,)), dma((16,)), dma((TERMS,)), dma((15,)),
        ],
        compiler_params=pltpu.CompilerParams(
            collective_id=0, has_side_effects=True, vmem_limit_bytes=60 * 1024 * 1024
        ),
    )(
        sizes, inner, ham, dip, amps.T, chan.reshape(1, channels), outer, energy, laser,
    )
    return pl.pallas_call(
        deliver,
        out_shape=(
            jax.ShapeDtypeStruct(inner.shape, F32),
            jax.ShapeDtypeStruct(outer.shape, F32),
        ),
        in_specs=[pl.BlockSpec(memory_space=pltpu.VMEM)] * 2,
        out_specs=(anywhere, anywhere),
        scratch_shapes=[dma((3,))],
        compiler_params=pltpu.CompilerParams(vmem_limit_bytes=1024 * 1024),
    )(*results)


def solution(mesh):
    placed = (
        P("sym", None, "dev"),
        P(),
        P("sym", "dev", None),
        P("sym", "dev", None),
        P(None, "dev"),
        P(),
        P(None, None, ("sym", "dev")),
        P(),
        P(),
    )
    return jax.shard_map(
        on_device,
        mesh=mesh,
        in_specs=placed,
        out_specs=(P("sym", None, "dev"), P(None, None, ("sym", "dev"))),
        check_vma=False,
    )
```
